512 devices in a mesh: ka: 16 (over y, core), op: 4 (over x), row: 8 (over z).
Axes of the slice: x: 4, y: 8, z: 8, core: 2. Of those that a mesh axis runs over, the one named last changes fastest.
Arguments:
- kgrid: int32 [3, 4096], P(None, ('ka', 'op', 'row')), may hold values from 0 to 63
- rvec: int32 [3, 256], replicated, may hold values from -8 to 8
- degen: int32 [256], replicated, may hold values from 1 to 4
- operators: bfloat16 [4, 256, 12800], P('op', ('ka', 'row')), may hold values from -1 to 1
- vectors: bfloat16 [4096, 12800], P(('ka', 'op', 'row')), may hold values from -0.5 to 0.5
Outputs:
- density: float32 [3, 4096], P(None, ('ka', 'op', 'row'))
- magnetization: float32 [3], replicated
The draws below stay inside these ranges and needn't reach their ends.
All inputs are finite; a program needn't handle non-finite values.
Results may differ from the reference program's by a relative error of at most 0.012.
Values may be sent and summed in bfloat16 or wider, within the bound.
A program may use at most 64 MiB of HBM per device.

```python
import math
import jax
import jax.numpy as jnp
from jax import lax

W = 80
GRID = 64
NR = 256
KPT = 8
KPOINTS = 4096


def draw_operators(key, part):
    base = jax.random.normal(jax.random.fold_in(key, 11), (4, NR, 2 * W * W), jnp.float32)
    spread = 1.5 / math.sqrt(NR)
    return jnp.clip(base * spread, -1.0, 1.0).astype(jnp.bfloat16)


def place_ends(entries, stream_key, smallest, top_value):
    index_at = [jax.random.randint(jax.random.fold_in(stream_key, axis), (), 0, length) for axis, length in enumerate(entries.shape)]
    main_axis = entries.shape.index(max(entries.shape))
    neighbour = index_at[:main_axis] + [(index_at[main_axis] + 1) % entries.shape[main_axis]] + index_at[main_axis + 1:]
    return entries.at[tuple(index_at)].set(smallest).at[tuple(neighbour)].set(top_value)


def block_scale(key, dims, cuts, smallest, largest):
    loudness = 1.0
    for dim, parts in cuts:
        draws = jax.random.uniform(jax.random.fold_in(jax.random.fold_in(key, 6), dim), (parts,), jnp.float32, smallest / len(cuts), largest / len(cuts))
        loudness = loudness * jnp.repeat(jnp.exp(draws), dims[dim] // parts).reshape((-1,) + (1,) * (len(dims) - 1 - dim))
    return loudness


def scatter_about(own_key, extent, deviation, most, split=(), kind=jnp.bfloat16):
    result = deviation * jax.random.normal(own_key, extent, jnp.float32)
    if split:
        result = result * block_scale(own_key, extent, split, -0.22, 0.18)
    return jnp.clip(result, -most, most).astype(kind)


def setup_inputs(seed: int = 0) -> dict:
    seeds = jax.random.split(jax.random.key(seed), 6)
    kgrid = place_ends(jax.random.randint(seeds[0], (3, KPOINTS), 0, GRID), jax.random.fold_in(seeds[0], 1), 0, GRID - 1).astype(jnp.int32)
    rvec = place_ends(jax.random.randint(seeds[1], (3, NR), -8, 9), jax.random.fold_in(seeds[1], 1), -8, 8).astype(jnp.int32)
    degen = place_ends(jax.random.randint(seeds[2], (NR,), 1, 5), jax.random.fold_in(seeds[2], 1), 1, 4).astype(jnp.int32)
    operators = draw_operators(jax.random.fold_in(seeds[5], 71), 0)
    vectors = scatter_about(seeds[4], (KPOINTS, 2 * W * W), (2 * W) ** -0.5, 0.5, ((0, 512),))
    return dict(kgrid=kgrid, rvec=rvec, degen=degen, operators=operators, vectors=vectors)


SMEARING = 0.5


def phase_pair(points, lattice, weights):
    winding = points[0][:, None] * lattice[0][None, :] + points[1][:, None] * lattice[1][None, :] + points[2][:, None] * lattice[2][None, :]
    winding = jnp.mod(winding, GRID)
    angle = (2.0 * math.pi / GRID) * winding.astype(jnp.float32)
    inverse = 1.0 / weights.astype(jnp.float32)
    cosine = (jnp.cos(angle) * inverse[None, :]).astype(jnp.bfloat16)
    sine = (jnp.sin(angle) * inverse[None, :]).astype(jnp.bfloat16)
    return cosine, sine


def transform(points, matrices, rvec, degen):
    cosine, sine = phase_pair(points, rvec, degen)
    cosine = cosine.astype(jnp.float32)
    sine = sine.astype(jnp.float32)
    half = matrices.shape[2] // 2
    real_in = matrices[:, :, :half].astype(jnp.float32)
    imag_in = matrices[:, :, half:].astype(jnp.float32)

    def mix(table, block):
        return jnp.einsum("kr,orx->okx", table, block)

    real_k = (mix(cosine, real_in) - mix(sine, imag_in)).astype(jnp.bfloat16)
    imag_k = (mix(cosine, imag_in) + mix(sine, real_in)).astype(jnp.bfloat16)
    return real_k, imag_k


def rotate_all(real_k, imag_k, vec_real, vec_imag):
    op_real = real_k.astype(jnp.float32)
    op_imag = imag_k.astype(jnp.float32)
    vr = vec_real.astype(jnp.float32)
    vi = vec_imag.astype(jnp.float32)
    prod_real = (jnp.einsum("okij,kjn->okin", op_real, vr) - jnp.einsum("okij,kjn->okin", op_imag, vi)).astype(jnp.bfloat16).astype(jnp.float32)
    prod_imag = (jnp.einsum("okij,kjn->okin", op_real, vi) + jnp.einsum("okij,kjn->okin", op_imag, vr)).astype(jnp.bfloat16).astype(jnp.float32)
    rot_real = (jnp.einsum("kin,okim->oknm", vr, prod_real) + jnp.einsum("kin,okim->oknm", vi, prod_imag)).astype(jnp.bfloat16)
    rot_imag = (jnp.einsum("kin,okim->oknm", vr, prod_imag) - jnp.einsum("kin,okim->oknm", vi, prod_real)).astype(jnp.bfloat16)
    return rot_real, rot_imag


def density_terms(rot_real, rot_imag):
    ham_real = rot_real[0].astype(jnp.float32)
    ham_imag = rot_imag[0].astype(jnp.float32)
    conn_real = rot_real[1:].astype(jnp.float32)
    conn_imag = rot_imag[1:].astype(jnp.float32)
    levels = jnp.diagonal(ham_real, axis1=1, axis2=2)
    filled = jax.nn.sigmoid(-levels / SMEARING)
    vacant = 1.0 - filled
    prod_real = jnp.einsum("knm,bkml->bknl", ham_real, conn_real) - jnp.einsum("knm,bkml->bknl", ham_imag, conn_imag)
    prod_imag = jnp.einsum("knm,bkml->bknl", ham_real, conn_imag) + jnp.einsum("knm,bkml->bknl", ham_imag, conn_real)
    weight = filled[None, :, :, None] * vacant[None, :, None, :]
    left_real = conn_real * weight
    left_imag = conn_imag * weight
    traces = jnp.einsum("aknm,bkmn->abk", left_real, prod_imag, precision=lax.Precision.HIGHEST) + jnp.einsum("aknm,bkmn->abk", left_imag, prod_real, precision=lax.Precision.HIGHEST)
    density = jnp.stack([traces[1, 2] - traces[2, 1], traces[2, 0] - traces[0, 2], traces[0, 1] - traces[1, 0]])
    return density / W


def reference(kgrid, rvec, degen, operators, vectors):
    blocks_count = KPOINTS // KPT
    blocks = kgrid.reshape(3, blocks_count, KPT).transpose(1, 0, 2)
    vector_blocks = vectors.reshape(blocks_count, KPT, 2, W, W)

    def block_density(bundle):
        points, vec = bundle
        real_k, imag_k = transform(points, operators, rvec, degen)
        real_k = real_k.reshape(4, KPT, W, W)
        imag_k = imag_k.reshape(4, KPT, W, W)
        rot_real, rot_imag = rotate_all(real_k, imag_k, vec[:, 0], vec[:, 1])
        return density_terms(rot_real, rot_imag)

    pieces = lax.map(block_density, (blocks, vector_blocks))
    density = pieces.transpose(1, 0, 2).reshape(3, KPOINTS)
    magnetization = jnp.sum(density, axis=1) / KPOINTS
    return density, magnetization
```

```python
import functools
import math

import jax
import jax.numpy as jnp
from jax import lax
from jax.experimental import pallas as pl
from jax.experimental.pallas import tpu as pltpu
from jax.sharding import PartitionSpec as P

W = 80
GRID = 64
SMEARING = 0.5
NX, NY, NZ, NC = 4, 8, 8, 2
XC = NX * NC
RING = 8
KPT = 8
NR = 256
HALF = W * W
CHUNK = 256
CHUNKS = HALF // CHUNK
FIRST_Q = 13
KPOINTS = 4096
MESH = pl.DeviceIdType.MESH
BF = jnp.bfloat16
F32 = jnp.float32


def place():
    ka = lax.axis_index("ka")
    return lax.axis_index("op"), lax.div(ka, 2), lax.rem(ka, 2), lax.axis_index("row")


def at(x, y, c, z):
    return (2 * y + c, x, z)


def held_p(c, z):
    live = (c == 0) | (lax.rem(z, 2) == 0) | (z == 7)
    return live, jnp.where(c == 0, z, 8 + lax.div(z + 1, 2))


def held_q(c, y):
    live = (c == 1) | (lax.rem(y, 2) == 0)
    return live, FIRST_Q + jnp.where(c == 1, y, 8 + lax.div(y, 2))


def settle(ref, sem):
    pltpu.make_async_copy(ref, ref, sem).wait()


def push(src, dst, send_sem, recv_sem, device):
    pltpu.make_async_remote_copy(
        src_ref=src, dst_ref=dst, send_sem=send_sem, recv_sem=recv_sem,
        device_id=device, device_id_type=MESH,
    ).start()


def keep(src, dst, sem):
    pltpu.make_async_copy(src, dst, sem).start()


def each(count, body):
    def step(i, carry):
        body(i)
        return carry

    lax.fori_loop(0, count, step, 0)


def iota(shape, dim):
    return lax.broadcasted_iota(jnp.int32, shape, dim)


def dot(a, b):
    return jnp.dot(a, b, preferred_element_type=F32)


def matrix_rows(tile, put):
    lane = iota((KPT, 128), 1)
    for i in range(W):
        first, off = divmod(i * W, 128)
        row = tile(first)
        if off:
            row = pltpu.roll(row, 128 - off, 1)
            if off + W > 128:
                nxt = pltpu.roll(tile(first + 1), 128 - off, 1)
                row = jnp.where(lane < 128 - off, row, nxt)
        put(i, jnp.where(lane < W, row, 0.0))


def fold_table(rows_ref, lattice, inverse, table):
    points = rows_ref[:, 0, :]
    spread = (lax.div(iota((512, 64), 0), 8) == iota((512, 64), 1)).astype(F32).astype(BF)
    wide = dot(spread, points.astype(BF))
    own = lax.rem(iota((512, 128), 0), 8) == lax.rem(iota((512, 128), 1), 8)
    wide = jnp.where(own, wide, 0.0).astype(BF)
    for part in range(4):
        winding = dot(wide[part * 128:(part + 1) * 128], lattice)
        winding = winding - GRID * jnp.floor(winding * (1.0 / GRID))
        upper = winding >= GRID // 2
        turn = jnp.where(upper, winding - (GRID // 2), winding) - (GRID // 4)
        sign = jnp.where(upper, -inverse, inverse)
        angle = turn * (2.0 * math.pi / GRID)
        sq = angle * angle
        odd = -1.0 / 39916800.0
        for term in (1.0 / 362880.0, -1.0 / 5040.0, 1.0 / 120.0, -1.0 / 6.0, 1.0):
            odd = odd * sq + term
        even = 1.0 / 479001600.0
        for term in (-1.0 / 3628800.0, 1.0 / 40320.0, -1.0 / 720.0, 1.0 / 24.0, -0.5, 1.0):
            even = even * sq + term
        table[part * 128:(part + 1) * 128, :NR] = (-odd * angle * sign).astype(BF)
        table[part * 128:(part + 1) * 128, NR:] = (even * sign).astype(BF)


def transform(table, gathered, out):
    for part in range(4):
        rows = slice(part * 128, (part + 1) * 128)
        block = gathered[...].reshape(NR, 2 * CHUNK)
        turned = jnp.concatenate([-block[:, CHUNK:], block[:, :CHUNK]], axis=1)
        total = dot(table[rows, :NR], block) + dot(table[rows, NR:], turned)
        out[part * 16:(part + 1) * 16] = total.reshape(16, KPT, 2 * CHUNK).astype(BF)


def body(
    kgrid, rvec, degen, operators, vectors, density, magnet,
    vec, own_row, k_p, k_q, in_p, in_q, stage, all_p, all_q, tab_p, tab_q,
    out_p, out_q, full, mats, right, left, sums,
    send1, send2, send3, k1_sem, k2_sem, in_sem, all_sem, full_sem, vec_sem, sum_send, sum_sem,
):
    x, y, c, z = place()
    xc = 2 * x + c
    live_p, chunk_p = held_p(c, z)
    live_q, chunk_q = held_q(c, y)
    barrier = pltpu.get_barrier_semaphore()
    keep(vectors, vec, vec_sem)

    def greet(i):
        px, pc, ring = lax.div(i, 16), lax.rem(lax.div(i, 8), 2), lax.rem(i, 8)
        same = (px == x) & (pc == c)

        @pl.when(jnp.logical_not(same & (ring == z)))
        def _():
            pl.semaphore_signal(barrier, inc=1, device_id=at(px, y, pc, ring), device_id_type=MESH)

        @pl.when(ring != y)
        def _():
            pl.semaphore_signal(barrier, inc=1, device_id=at(px, ring, pc, z), device_id_type=MESH)

    each(64, greet)

    stage[...] = jnp.zeros_like(stage)
    stage[0:3, 0:KPT] = kgrid[...].astype(F32)
    row = stage[0:1, 0:128]
    row = row + pltpu.roll(stage[1:2, 0:128], 8, 1) + pltpu.roll(stage[2:3, 0:128], 16, 1)
    own_row[0] = row
    k_p[xc * 8 + z] = row
    k_q[xc * 8 + y] = row

    pl.semaphore_wait(barrier, 63 + 56)

    def share_points(i):
        @pl.when(i != z)
        def _():
            push(own_row.at[0], k_p.at[xc * 8 + z], send1, k1_sem.at[0], at(x, y, c, i))

        @pl.when(i != y)
        def _():
            push(own_row.at[0], k_q.at[xc * 8 + y], send1, k1_sem.at[1], at(x, i, c, z))

    each(RING, share_points)

    def pieces(chunk, dst, sem, device, local):
        for part in range(2):
            col = pl.multiple_of(part * HALF + chunk * CHUNK, 128)
            src = operators.at[0, :, pl.ds(col, CHUNK)]
            if local:
                keep(src, dst.at[part], sem)
            else:
                push(src, dst.at[part], send2, sem, device)

    def share_columns(i):
        pc, ring = lax.div(i, 8), lax.rem(i, 8)
        live, chunk = held_p(pc, ring)
        me = (pc == c) & (ring == z)

        @pl.when(live & me)
        def _():
            pieces(chunk, in_p.at[c * 8 + z], in_sem.at[0], None, True)

        @pl.when(live & jnp.logical_not(me))
        def _():
            pieces(chunk, in_p.at[c * 8 + z], in_sem.at[0], at(x, y, pc, ring), False)

        live2, chunk2 = held_q(pc, ring)
        me2 = (pc == c) & (ring == y)

        @pl.when(live2 & me2)
        def _():
            pieces(chunk2, in_q.at[c * 8 + y], in_sem.at[1], None, True)

        @pl.when(live2 & jnp.logical_not(me2))
        def _():
            pieces(chunk2, in_q.at[c * 8 + y], in_sem.at[1], at(x, ring, pc, z), False)

    each(16, share_columns)

    settle(k_p.at[pl.ds(0, 7)], k1_sem.at[0])
    settle(k_q.at[pl.ds(0, 7)], k1_sem.at[1])

    def share_rows(i):
        px, pc = lax.div(i, 2), lax.rem(i, 2)

        @pl.when(i != xc)
        def _():
            push(k_p.at[pl.ds(xc * 8, 8)], k_p.at[pl.ds(xc * 8, 8)], send1, k2_sem.at[0], at(px, y, pc, z))
            push(k_q.at[pl.ds(xc * 8, 8)], k_q.at[pl.ds(xc * 8, 8)], send1, k2_sem.at[1], at(px, y, pc, z))

    each(XC, share_rows)

    def collect(incoming, gathered, slot, sem, gather_sem, along_y):
        settle(incoming, sem)
        for s in range(16):
            for part in range(2):
                stage[2 * s:2 * s + 2, part * CHUNK:(part + 1) * CHUNK] = incoming[s, part].astype(F32)
        gathered[slot] = stage[...].astype(BF)

        def spread(i):
            @pl.when(i != slot)
            def _():
                device = at(x, i, c, z) if along_y else at(x, y, c, i)
                push(gathered.at[slot], gathered.at[slot], send3, gather_sem, device)

        each(RING, spread)

    @pl.when(live_p)
    def _():
        collect(in_p, all_p, y, in_sem.at[0], all_sem.at[0], True)

    @pl.when(live_q)
    def _():
        collect(in_q, all_q, z, in_sem.at[1], all_sem.at[1], False)

    pltpu.make_async_copy(vectors, vec, vec_sem).wait()
    for part in range(2):
        def put(i, val, part=part):
            mats[part, i * KPT:(i + 1) * KPT, :] = val

        matrix_rows(lambda t, part=part: vec[:, part * HALF + t * 128: part * HALF + (t + 1) * 128].astype(F32), put)

    lane = iota((W, 128), 1)

    def eigen(k):
        vr = mats[0, pl.ds(k, W, stride=KPT), :]
        vi = mats[1, pl.ds(k, W, stride=KPT), :]
        gap = jnp.zeros((48, 256), BF)
        right[k, 0:W, :] = jnp.concatenate([vr, vi], axis=1).astype(BF)
        right[k, W:128, :] = gap
        right[k, 128:128 + W, :] = jnp.concatenate([-vi, vr], axis=1).astype(BF)
        right[k, 128 + W:, :] = gap
        fill = jnp.zeros((48, 128), F32)
        tr = jnp.transpose(jnp.concatenate([vr, fill], axis=0))[:W]
        ti = jnp.transpose(jnp.concatenate([vi, fill], axis=0))[:W]
        left[k] = paired(tr, ti).astype(BF)

    def paired(re, im):
        moved = pltpu.roll(im, W, 1)
        return jnp.concatenate([jnp.where(lane < W, re, moved), jnp.where(lane < 2 * W - 128, moved, 0.0)], axis=1)

    each(KPT, eigen)

    settle(k_p.at[pl.ds(0, 56)], k2_sem.at[0])
    settle(k_q.at[pl.ds(0, 56)], k2_sem.at[1])
    lattice_rows = iota((128, NR), 0)
    rv = rvec[...].astype(F32)
    lattice = jnp.where(
        lattice_rows < 8, rv[0:1],
        jnp.where(lattice_rows < 16, rv[1:2], jnp.where(lattice_rows < 24, rv[2:3], 0.0)),
    )
    weight = degen[...].astype(F32)

    @pl.when(live_p)
    def _():
        fold_table(k_p, lattice.astype(BF), 1.0 / weight, tab_p)

    @pl.when(live_q)
    def _():
        col = iota((NR, NR), 1)
        source = (
            lax.rem(lax.div(col, 2), 8) * 32 + lax.rem(lax.div(col, 16), 2) * 16
            + lax.div(col, 32) * 2 + lax.rem(col, 2)
        )
        swap = (iota((NR, NR), 0) == source).astype(F32).astype(BF)
        moved = dot(lattice.astype(BF), swap).astype(BF)
        weights = dot(jnp.broadcast_to(weight, (8, NR)).astype(BF), swap)[0:1]
        fold_table(k_q, moved, 1.0 / weights, tab_q)

    def deliver(chunk, out, along_z):
        def one(i):
            px, pc, ring = lax.div(i, 16), lax.rem(lax.div(i, 8), 2), lax.rem(i, 8)
            me = (px == x) & (pc == c) & (ring == (z if along_z else y))
            dst = full.at[x, chunk]
            device = at(px, y, pc, ring) if along_z else at(px, ring, pc, z)

            @pl.when(me)
            def _():
                keep(out.at[i], dst, full_sem)

            @pl.when(jnp.logical_not(me))
            def _():
                push(out.at[i], dst, send3, full_sem, device)

        each(64, one)

    @pl.when(live_p)
    def _():
        settle(all_p.at[pl.ds(0, 7)], all_sem.at[0])
        transform(tab_p, all_p, out_p)
        deliver(chunk_p, out_p, True)

    @pl.when(live_q)
    def _():
        settle(all_q.at[pl.ds(0, 7)], all_sem.at[1])
        transform(tab_q, all_q, out_q)
        deliver(chunk_q, out_q, False)

    settle(full, full_sem)

    def rebuild(o):
        for part in range(2):
            def put(i, val, part=part):
                mats[2 * o + part, i * KPT:(i + 1) * KPT, :] = val

            matrix_rows(
                lambda t, part=part: full[o, t // 2, :, part * CHUNK + (t % 2) * 128: part * CHUNK + (t % 2 + 1) * 128].astype(F32),
                put,
            )

    each(4, rebuild)

    sub = iota((W, 128), 0)
    density_lane = iota((1, 128), 1)

    def point(k, carry):
        ops = [
            jnp.concatenate(
                [mats[2 * o, pl.ds(k, W, stride=KPT), :], mats[2 * o + 1, pl.ds(k, W, stride=KPT), :]], axis=1
            ).astype(BF)
            for o in range(4)
        ]
        prod = dot(jnp.concatenate(ops, axis=0), right[k])
        turn = left[k][:, :256]
        rot = []
        for o in range(4):
            re = prod[o * W:(o + 1) * W, :128]
            im = prod[o * W:(o + 1) * W, 128:]
            stacked = jnp.concatenate(
                [jnp.concatenate([re, im], axis=1), jnp.concatenate([im, -re], axis=1), jnp.zeros((96, 256), F32)],
                axis=0,
            ).astype(BF)
            rot.append(dot(turn, stacked).astype(BF).astype(F32))
        ham_re, ham_im = rot[0][:, :128], rot[0][:, 128:]
        diag = jnp.where(sub == lane, ham_re, 0.0)
        down = 1.0 / (1.0 + jnp.exp(jnp.sum(diag, axis=1, keepdims=True) * (1.0 / SMEARING)))
        along = 1.0 / (1.0 + jnp.exp(jnp.sum(diag, axis=0, keepdims=True) * (1.0 / SMEARING)))
        weight2 = (1.0 - down) * along
        ham = paired(ham_re, ham_im).astype(BF)
        prods, turned = [], []
        fill = jnp.zeros((48, 128), F32)
        for b in range(3):
            re, im = rot[b + 1][:, :128], rot[b + 1][:, 128:]
            stacked = jnp.concatenate(
                [jnp.concatenate([re, im], axis=1), jnp.concatenate([-im, re], axis=1), jnp.zeros((96, 256), F32)],
                axis=0,
            ).astype(BF)
            prods.append(dot(ham, stacked))
            turned.append((
                jnp.transpose(jnp.concatenate([re, fill], axis=0))[:W] * weight2,
                jnp.transpose(jnp.concatenate([im, fill], axis=0))[:W] * weight2,
            ))
        for comp, (a, b) in enumerate(((1, 2), (2, 0), (0, 1))):
            terms = (
                turned[a][0] * prods[b][:, 128:] + turned[a][1] * prods[b][:, :128]
                - turned[b][0] * prods[a][:, 128:] - turned[b][1] * prods[a][:, :128]
            )
            total = jnp.sum(jnp.sum(terms, axis=0, keepdims=True), axis=1, keepdims=True) * (1.0 / W)
            stage[comp:comp + 1, 0:128] = stage[comp:comp + 1, 0:128] + jnp.where(density_lane == k, total, 0.0)
        return carry

    stage[0:8, 0:128] = jnp.zeros((8, 128), F32)
    lax.fori_loop(0, KPT, point, 0)
    dens = stage[0:8, 0:128]
    density[...] = dens[0:3, 0:KPT]

    total = jnp.sum(dens, axis=1, keepdims=True)
    eye = iota((8, 128), 0) == iota((8, 128), 1)
    part = jnp.sum(jnp.where(eye, total, 0.0), axis=0, keepdims=True)
    for level in range(3):
        slot = (xc, z, y)[level]
        sums[level, slot] = part

        def tell(i, level=level, slot=slot):
            px, pc = lax.div(i, 2), lax.rem(i, 2)
            device = (at(px, y, pc, z), at(x, y, c, i), at(x, i, c, z))[level]

            @pl.when(i != slot)
            def _():
                push(sums.at[level, slot], sums.at[level, slot], sum_send, sum_sem.at[level], device)

        each(8, tell)
        settle(sums.at[level, pl.ds(0, 7)], sum_sem.at[level])
        part = jnp.sum(sums[level, :, 0, :], axis=0, keepdims=True)
    magnet[...] = part[:, 0:3] * (1.0 / KPOINTS)

    for level in range(3):
        settle(sums.at[level, pl.ds(0, 7)], sum_send)
    settle(k_p.at[pl.ds(0, 14)], send1)
    settle(k_p.at[pl.ds(0, 56)], send1)
    settle(k_p.at[pl.ds(0, 56)], send1)

    settle(in_p.at[pl.ds(0, 12)], send2)

    @pl.when(jnp.logical_not(live_p))
    def _():
        settle(in_p.at[pl.ds(0, 1)], send2)

    settle(in_q.at[pl.ds(0, 11)], send2)

    @pl.when(jnp.logical_not(live_q))
    def _():
        settle(in_q.at[pl.ds(0, 1)], send2)

    @pl.when(live_p)
    def _():
        settle(all_p.at[pl.ds(0, 7)], send3)
        settle(out_p.at[pl.ds(0, 63)], send3)

    @pl.when(live_q)
    def _():
        settle(all_q.at[pl.ds(0, 7)], send3)
        settle(out_q.at[pl.ds(0, 63)], send3)


def per_device(kgrid, rvec, degen, operators, vectors):
    vmem = pl.BlockSpec(memory_space=pltpu.VMEM)
    anywhere = pl.BlockSpec(memory_space=pl.ANY)
    dma = pltpu.SemaphoreType.DMA
    density, magnet = pl.pallas_call(
        body,
        out_shape=(jax.ShapeDtypeStruct((3, KPT), F32), jax.ShapeDtypeStruct((1, 3), F32)),
        in_specs=[vmem, vmem, vmem, anywhere, anywhere],
        out_specs=(vmem, vmem),
        scratch_shapes=[
            pltpu.VMEM((KPT, 2 * HALF), BF),
            pltpu.VMEM((1, 1, 128), F32),
            pltpu.VMEM((64, 1, 128), F32),
            pltpu.VMEM((64, 1, 128), F32),
            pltpu.VMEM((16, 2, 2, CHUNK), BF),
            pltpu.VMEM((16, 2, 2, CHUNK), BF),
            pltpu.VMEM((32, 2 * CHUNK), F32),
            pltpu.VMEM((RING, 32, 2 * CHUNK), BF),
            pltpu.VMEM((RING, 32, 2 * CHUNK), BF),
            pltpu.VMEM((512, 2 * NR), BF),
            pltpu.VMEM((512, 2 * NR), BF),
            pltpu.VMEM((64, KPT, 2 * CHUNK), BF),
            pltpu.VMEM((64, KPT, 2 * CHUNK), BF),
            pltpu.VMEM((4, CHUNKS, KPT, 2 * CHUNK), BF),
            pltpu.VMEM((8, W * KPT, 128), F32),
            pltpu.VMEM((KPT, 256, 256), BF),
            pltpu.VMEM((KPT, W, 256), BF),
            pltpu.VMEM((3, 8, 1, 128), F32),
            dma, dma, dma, dma((2,)), dma((2,)), dma((2,)), dma((2,)), dma, dma, dma, dma((3,)),
        ],
        compiler_params=pltpu.CompilerParams(
            collective_id=0, has_side_effects=True, vmem_limit_bytes=56 * 1024 * 1024
        ),
        name="orbital",
    )(kgrid, rvec, degen.reshape(1, NR), operators, vectors)
    return density, magnet.reshape(3)


def solution(mesh):
    return jax.shard_map(
        per_device,
        mesh=mesh,
        in_specs=(P(None, ("ka", "op", "row")), P(), P(), P("op", ("ka", "row"), None), P(("ka", "op", "row"), None)),
        out_specs=(P(None, ("ka", "op", "row")), P()),
        check_vma=False,
    )
```

```python
import functools
import math

import jax
import jax.numpy as jnp
from jax import lax
from jax.experimental import pallas as pl
from jax.experimental.pallas import tpu as pltpu
from jax.sharding import PartitionSpec as P

W = 80
GRID = 64
SMEARING = 0.5
NX, NY, NZ, NC = 4, 8, 8, 2
XC = NX * NC
RING = 8
KPT = 8
NR = 256
HALF = W * W
CHUNK = 256
CHUNKS = HALF // CHUNK
FIRST_Q = 13
KPOINTS = 4096
TOGETHER = 2
MESH = pl.DeviceIdType.MESH
BF = jnp.bfloat16
F32 = jnp.float32


def place():
    ka = lax.axis_index("ka")
    return lax.axis_index("op"), lax.div(ka, 2), lax.rem(ka, 2), lax.axis_index("row")


def at(x, y, c, z):
    return (2 * y + c, x, z)


def held_p(c, z):
    live = (c == 0) | (lax.rem(z, 2) == 0) | (z == 7)
    return live, jnp.where(c == 0, z, 8 + lax.div(z + 1, 2))


def held_q(c, y):
    live = (c == 1) | (lax.rem(y, 2) == 0)
    return live, FIRST_Q + jnp.where(c == 1, y, 8 + lax.div(y, 2))


FAR = (4, 3, 5, 2, 6, 1, 7)


def settle(ref, sem):
    pltpu.make_async_copy(ref, ref, sem).wait()


def push(src, dst, send_sem, recv_sem, device):
    pltpu.make_async_remote_copy(
        src_ref=src, dst_ref=dst, send_sem=send_sem, recv_sem=recv_sem,
        device_id=device, device_id_type=MESH,
    ).start()


def keep(src, dst, sem):
    pltpu.make_async_copy(src, dst, sem).start()


def each(count, body):
    def step(i, carry):
        body(i)
        return carry

    lax.fori_loop(0, count, step, 0)


def around(place, step):
    return lax.rem(place + step, RING)


def partners(x, c):
    order = ((2, 0), (2, 1), (1, 0), (3, 0), (1, 1), (3, 1), (0, 1), (0, 0))
    found = []
    for dx, dc in order:
        px, pc = lax.rem(x + dx, NX), (1 - c if dc else c)
        found.append((px, pc, 2 * px + pc))
    return found


def iota(shape, dim):
    return lax.broadcasted_iota(jnp.int32, shape, dim)


def dot(a, b):
    return jnp.dot(a, b, preferred_element_type=F32)


def matrix_rows(tile, put):
    lane = iota((KPT, 128), 1)
    for i in range(W):
        first, off = divmod(i * W, 128)
        row = tile(first)
        if off:
            row = pltpu.roll(row, 128 - off, 1)
            if off + W > 128:
                nxt = pltpu.roll(tile(first + 1), 128 - off, 1)
                row = jnp.where(lane < 128 - off, row, nxt)
        put(i, jnp.where(lane < W, row, 0.0))


def fold_table(rows_ref, lattice, inverse, table):
    points = rows_ref[:, 0, :]
    spread = (lax.div(iota((512, 64), 0), 8) == iota((512, 64), 1)).astype(F32).astype(BF)
    wide = dot(spread, points.astype(BF))
    own = lax.rem(iota((512, 128), 0), 8) == lax.rem(iota((512, 128), 1), 8)
    wide = jnp.where(own, wide, 0.0).astype(BF)
    for part in range(4):
        winding = dot(wide[part * 128:(part + 1) * 128], lattice)
        winding = winding - GRID * jnp.floor(winding * (1.0 / GRID))
        upper = winding >= GRID // 2
        turn = jnp.where(upper, winding - (GRID // 2), winding) - (GRID // 4)
        sign = jnp.where(upper, -inverse, inverse)
        angle = turn * (2.0 * math.pi / GRID)
        sq = angle * angle
        odd = -1.0 / 39916800.0
        for term in (1.0 / 362880.0, -1.0 / 5040.0, 1.0 / 120.0, -1.0 / 6.0, 1.0):
            odd = odd * sq + term
        even = 1.0 / 479001600.0
        for term in (-1.0 / 3628800.0, 1.0 / 40320.0, -1.0 / 720.0, 1.0 / 24.0, -0.5, 1.0):
            even = even * sq + term
        table[part * 128:(part + 1) * 128, :NR] = (-odd * angle * sign).astype(BF)
        table[part * 128:(part + 1) * 128, NR:] = (even * sign).astype(BF)


def transform(table, gathered, out):
    for part in range(4):
        rows = slice(part * 128, (part + 1) * 128)
        block = gathered[...].reshape(NR, 2 * CHUNK)
        turned = jnp.concatenate([-block[:, CHUNK:], block[:, :CHUNK]], axis=1)
        total = dot(table[rows, :NR], block) + dot(table[rows, NR:], turned)
        out[part * 16:(part + 1) * 16] = total.reshape(16, KPT, 2 * CHUNK).astype(BF)


def body(
    kgrid_hbm, rvec_hbm, degen_hbm, operators, vectors, density, magnet,
    kgrid, rvec, degen, vec, own_row, k_p, k_q, in_p, in_q, stage, all_p, all_q, tab_p, tab_q,
    out_p, out_q, full, mats, right, left, sums, sums2,
    send1, send2, send3, k1_sem, k2_sem, in_sem, all_sem, full_sem, vec_sem, sum_send, sum_sem, kg_sem, small_sem,
):
    x, y, c, z = place()
    xc = 2 * x + c
    live_p, chunk_p = held_p(c, z)
    live_q, chunk_q = held_q(c, y)
    barrier = pltpu.get_barrier_semaphore()
    keep(kgrid_hbm, kgrid, kg_sem)
    keep(rvec_hbm, rvec, small_sem.at[0])
    keep(degen_hbm, degen, small_sem.at[1])
    keep(vectors, vec, vec_sem)
    columns = partners(x, c)

    def greet(step):
        for px, pc, _ in columns:
            pl.semaphore_signal(barrier, inc=1, device_id=at(px, y, pc, around(z, step)), device_id_type=MESH)
            pl.semaphore_signal(barrier, inc=1, device_id=at(px, around(y, step), pc, z), device_id_type=MESH)

    for px, pc, _ in columns[:-1]:
        pl.semaphore_signal(barrier, inc=1, device_id=at(px, y, pc, z), device_id_type=MESH)
    each(7, lambda i: greet(i + 1))
    pltpu.make_async_copy(kgrid_hbm, kgrid, kg_sem).wait()

    stage[...] = jnp.zeros_like(stage)
    stage[0:3, 0:KPT] = kgrid[...].astype(F32)
    row = stage[0:1, 0:128]
    row = row + pltpu.roll(stage[1:2, 0:128], 8, 1) + pltpu.roll(stage[2:3, 0:128], 16, 1)
    own_row[0] = row
    k_p[xc * 8 + z] = row
    k_q[xc * 8 + y] = row

    pl.semaphore_wait(barrier, 63 + 56)

    for step in FAR:
        push(own_row.at[0], k_p.at[xc * 8 + z], send1, k1_sem.at[0], at(x, y, c, around(z, step)))
        push(own_row.at[0], k_q.at[xc * 8 + y], send1, k1_sem.at[1], at(x, around(y, step), c, z))

    def pieces(chunk, dst, sem, device, local):
        for part in range(2):
            col = pl.multiple_of(part * HALF + chunk * CHUNK, 128)
            src = operators.at[0, :, pl.ds(col, CHUNK)]
            if local:
                keep(src, dst.at[part], sem)
            else:
                push(src, dst.at[part], send2, sem, device)

    def offer(step, pc):
        ring = around(z, step)
        live, chunk = held_p(pc, ring)

        @pl.when(live)
        def _():
            pieces(chunk, in_p.at[c * 8 + z], in_sem.at[0], at(x, y, pc, ring), False)

        ring2 = around(y, step)
        live2, chunk2 = held_q(pc, ring2)

        @pl.when(live2)
        def _():
            pieces(chunk2, in_q.at[c * 8 + y], in_sem.at[1], at(x, ring2, pc, z), False)

    for step in FAR:
        offer(step, c)
        offer(step, 1 - c)
    offer(0, 1 - c)

    @pl.when(live_p)
    def _():
        pieces(chunk_p, in_p.at[c * 8 + z], in_sem.at[0], None, True)

    @pl.when(live_q)
    def _():
        pieces(chunk_q, in_q.at[c * 8 + y], in_sem.at[1], None, True)

    settle(k_p.at[pl.ds(0, 7)], k1_sem.at[0])
    settle(k_q.at[pl.ds(0, 7)], k1_sem.at[1])

    for px, pc, _ in columns[:-1]:
        push(k_p.at[pl.ds(xc * 8, 8)], k_p.at[pl.ds(xc * 8, 8)], send1, k2_sem.at[0], at(px, y, pc, z))
        push(k_q.at[pl.ds(xc * 8, 8)], k_q.at[pl.ds(xc * 8, 8)], send1, k2_sem.at[1], at(px, y, pc, z))

    def collect(incoming, gathered, slot, sem, gather_sem, along_y):
        settle(incoming, sem)
        for s in range(16):
            for part in range(2):
                stage[2 * s:2 * s + 2, part * CHUNK:(part + 1) * CHUNK] = incoming[s, part].astype(F32)
        gathered[slot] = stage[...].astype(BF)

        for step in FAR:
            device = at(x, around(y, step), c, z) if along_y else at(x, y, c, around(z, step))
            push(gathered.at[slot], gathered.at[slot], send3, gather_sem, device)

    @pl.when(live_p)
    def _():
        collect(in_p, all_p, y, in_sem.at[0], all_sem.at[0], True)

    @pl.when(live_q)
    def _():
        collect(in_q, all_q, z, in_sem.at[1], all_sem.at[1], False)

    pltpu.make_async_copy(vectors, vec, vec_sem).wait()
    for part in range(2):
        def put(i, val, part=part):
            mats[part, i * KPT:(i + 1) * KPT, :] = val

        matrix_rows(lambda t, part=part: vec[:, part * HALF + t * 128: part * HALF + (t + 1) * 128].astype(F32), put)

    lane = iota((W, 128), 1)

    def eigen(k):
        vr = mats[0, pl.ds(k, W, stride=KPT), :]
        vi = mats[1, pl.ds(k, W, stride=KPT), :]
        gap = jnp.zeros((48, 256), BF)
        right[k, 0:W, :] = jnp.concatenate([vr, vi], axis=1).astype(BF)
        right[k, W:128, :] = gap
        right[k, 128:128 + W, :] = jnp.concatenate([-vi, vr], axis=1).astype(BF)
        right[k, 128 + W:, :] = gap
        fill = jnp.zeros((48, 128), F32)
        tr = jnp.transpose(jnp.concatenate([vr, fill], axis=0))[:W]
        ti = jnp.transpose(jnp.concatenate([vi, fill], axis=0))[:W]
        left[k] = paired(tr, ti).astype(BF)

    def paired(re, im):
        moved = pltpu.roll(im, W, 1)
        return jnp.concatenate([jnp.where(lane < W, re, moved), moved[:, :2 * W - 128]], axis=1)

    each(KPT, eigen)

    pltpu.make_async_copy(rvec_hbm, rvec, small_sem.at[0]).wait()
    pltpu.make_async_copy(degen_hbm, degen, small_sem.at[1]).wait()
    settle(k_p.at[pl.ds(0, 56)], k2_sem.at[0])
    settle(k_q.at[pl.ds(0, 56)], k2_sem.at[1])
    lattice_rows = iota((128, NR), 0)
    rv = rvec[...].astype(F32)
    lattice = jnp.where(
        lattice_rows < 8, rv[0:1],
        jnp.where(lattice_rows < 16, rv[1:2], jnp.where(lattice_rows < 24, rv[2:3], 0.0)),
    )
    weight = degen[...].astype(F32)

    @pl.when(live_p)
    def _():
        fold_table(k_p, lattice.astype(BF), 1.0 / weight, tab_p)

    @pl.when(live_q)
    def _():
        col = iota((NR, NR), 1)
        source = (
            lax.rem(lax.div(col, 2), 8) * 32 + lax.rem(lax.div(col, 16), 2) * 16
            + lax.div(col, 32) * 2 + lax.rem(col, 2)
        )
        swap = (iota((NR, NR), 0) == source).astype(F32).astype(BF)
        moved = dot(lattice.astype(BF), swap).astype(BF)
        weights = dot(jnp.broadcast_to(weight, (8, NR)).astype(BF), swap)[0:1]
        fold_table(k_q, moved, 1.0 / weights, tab_q)

    def deliver(chunk, out, along_z):
        dst = full.at[x, chunk]

        def one(step, some):
            ring = around(z if along_z else y, step)
            for px, pc, pxc in some:
                device = at(px, y, pc, ring) if along_z else at(px, ring, pc, z)
                push(out.at[pxc * 8 + ring], dst, send3, full_sem, device)

        def far(i):
            half = lax.div(i + 1, 2)
            one(jnp.where(lax.rem(i, 2) == 0, 4 + half, 4 - half), columns)

        each(7, far)
        one(0, columns[:-1])
        keep(out.at[xc * 8 + (z if along_z else y)], dst, full_sem)

    @pl.when(live_p)
    def _():
        settle(all_p.at[pl.ds(0, 7)], all_sem.at[0])
        transform(tab_p, all_p, out_p)
        deliver(chunk_p, out_p, True)

    @pl.when(live_q)
    def _():
        settle(all_q.at[pl.ds(0, 7)], all_sem.at[1])
        transform(tab_q, all_q, out_q)
        deliver(chunk_q, out_q, False)

    settle(full, full_sem)

    def rebuild(o):
        for part in range(2):
            def put(i, val, part=part):
                mats[2 * o + part, i * KPT:(i + 1) * KPT, :] = val

            matrix_rows(
                lambda t, part=part: full[o, t // 2, :, part * CHUNK + (t % 2) * 128: part * CHUNK + (t % 2 + 1) * 128].astype(F32),
                put,
            )

    each(4, rebuild)

    sub = iota((W, 128), 0)
    density_lane = iota((1, 128), 1)

    def point(k, carry):
        ops = [
            jnp.concatenate(
                [mats[2 * o, pl.ds(k, W, stride=KPT), :], mats[2 * o + 1, pl.ds(k, W, stride=KPT), :]], axis=1
            ).astype(BF)
            for o in range(4)
        ]
        prod = dot(jnp.concatenate(ops, axis=0), right[k])
        turn = left[k]
        rot = []
        for o in range(4):
            re = prod[o * W:(o + 1) * W, :128]
            im = prod[o * W:(o + 1) * W, 128:]
            stacked = jnp.concatenate(
                [jnp.concatenate([re, im], axis=1), jnp.concatenate([im, -re], axis=1)],
                axis=0,
            ).astype(BF)
            rot.append(dot(turn, stacked).astype(BF).astype(F32))
        ham_re, ham_im = rot[0][:, :128], rot[0][:, 128:]
        diag = jnp.where(sub == lane, ham_re, 0.0)
        down = 1.0 / (1.0 + jnp.exp(jnp.sum(diag, axis=1, keepdims=True) * (1.0 / SMEARING)))
        along = 1.0 / (1.0 + jnp.exp(jnp.sum(diag, axis=0, keepdims=True) * (1.0 / SMEARING)))
        weight2 = (1.0 - down) * along
        ham = paired(ham_re, ham_im).astype(BF)
        prods, turned = [], []
        fill = jnp.zeros((48, 128), F32)
        for b in range(3):
            re, im = rot[b + 1][:, :128], rot[b + 1][:, 128:]
            stacked = jnp.concatenate(
                [jnp.concatenate([re, im], axis=1), jnp.concatenate([-im, re], axis=1)],
                axis=0,
            ).astype(BF)
            prods.append(dot(ham, stacked))
            turned.append((
                jnp.transpose(jnp.concatenate([re, fill], axis=0))[:W] * weight2,
                jnp.transpose(jnp.concatenate([im, fill], axis=0))[:W] * weight2,
            ))
        for comp, (a, b) in enumerate(((1, 2), (2, 0), (0, 1))):
            terms = (
                turned[a][0] * prods[b][:, 128:] + turned[a][1] * prods[b][:, :128]
                - turned[b][0] * prods[a][:, 128:] - turned[b][1] * prods[a][:, :128]
            )
            total = jnp.sum(jnp.sum(terms, axis=0, keepdims=True), axis=1, keepdims=True) * (1.0 / W)
            stage[comp:comp + 1, 0:128] = stage[comp:comp + 1, 0:128] + jnp.where(density_lane == k, total, 0.0)
        return carry

    stage[0:8, 0:128] = jnp.zeros((8, 128), F32)
    def points(i, carry):
        for j in range(TOGETHER):
            carry = point(TOGETHER * i + j, carry)
        return carry

    lax.fori_loop(0, KPT // TOGETHER, points, 0)
    dens = stage[0:8, 0:128]
    density[...] = dens[0:3, 0:KPT]

    total = jnp.sum(dens, axis=1, keepdims=True)
    eye = iota((8, 128), 0) == iota((8, 128), 1)
    part = jnp.sum(jnp.where(eye, total, 0.0), axis=0, keepdims=True)
    sums[xc * 8 + z] = part

    def tell(step, some):
        ring = around(z, step)
        for px, pc, _ in some:
            push(sums.at[xc * 8 + z], sums.at[xc * 8 + z], sum_send, sum_sem.at[0], at(px, y, pc, ring))

    def tell_far(i):
        half = lax.div(i + 1, 2)
        tell(jnp.where(lax.rem(i, 2) == 0, 4 + half, 4 - half), columns)

    each(7, tell_far)
    tell(0, columns[:-1])
    settle(sums.at[pl.ds(0, 63)], sum_sem.at[0])
    sums2[y] = jnp.sum(sums[:, 0, :], axis=0, keepdims=True)
    for step in FAR:
        push(sums2.at[y], sums2.at[y], sum_send, sum_sem.at[1], at(x, around(y, step), c, z))
    settle(sums2.at[pl.ds(0, 7)], sum_sem.at[1])
    part = jnp.sum(sums2[:, 0, :], axis=0, keepdims=True)
    magnet[...] = part[:, 0:3] * (1.0 / KPOINTS)

    settle(sums.at[pl.ds(0, 63)], sum_send)
    settle(sums2.at[pl.ds(0, 7)], sum_send)
    settle(k_p.at[pl.ds(0, 14)], send1)
    settle(k_p.at[pl.ds(0, 56)], send1)
    settle(k_p.at[pl.ds(0, 56)], send1)

    settle(in_p.at[pl.ds(0, 12)], send2)

    @pl.when(jnp.logical_not(live_p))
    def _():
        settle(in_p.at[pl.ds(0, 1)], send2)

    settle(in_q.at[pl.ds(0, 11)], send2)

    @pl.when(jnp.logical_not(live_q))
    def _():
        settle(in_q.at[pl.ds(0, 1)], send2)

    @pl.when(live_p)
    def _():
        settle(all_p.at[pl.ds(0, 7)], send3)
        settle(out_p.at[pl.ds(0, 63)], send3)

    @pl.when(live_q)
    def _():
        settle(all_q.at[pl.ds(0, 7)], send3)
        settle(out_q.at[pl.ds(0, 63)], send3)


def per_device(kgrid, rvec, degen, operators, vectors):
    vmem = pl.BlockSpec(memory_space=pltpu.VMEM)
    anywhere = pl.BlockSpec(memory_space=pl.ANY)
    dma = pltpu.SemaphoreType.DMA
    density, magnet = pl.pallas_call(
        body,
        out_shape=(jax.ShapeDtypeStruct((3, KPT), F32), jax.ShapeDtypeStruct((1, 3), F32)),
        in_specs=[anywhere] * 5,
        out_specs=(vmem, vmem),
        scratch_shapes=[
            pltpu.VMEM((3, KPT), jnp.int32),
            pltpu.VMEM((3, NR), jnp.int32),
            pltpu.VMEM((1, NR), jnp.int32),
            pltpu.VMEM((KPT, 2 * HALF), BF),
            pltpu.VMEM((1, 1, 128), F32),
            pltpu.VMEM((64, 1, 128), F32),
            pltpu.VMEM((64, 1, 128), F32),
            pltpu.VMEM((16, 2, 2, CHUNK), BF),
            pltpu.VMEM((16, 2, 2, CHUNK), BF),
            pltpu.VMEM((32, 2 * CHUNK), F32),
            pltpu.VMEM((RING, 32, 2 * CHUNK), BF),
            pltpu.VMEM((RING, 32, 2 * CHUNK), BF),
            pltpu.VMEM((512, 2 * NR), BF),
            pltpu.VMEM((512, 2 * NR), BF),
            pltpu.VMEM((64, KPT, 2 * CHUNK), BF),
            pltpu.VMEM((64, KPT, 2 * CHUNK), BF),
            pltpu.VMEM((4, CHUNKS, KPT, 2 * CHUNK), BF),
            pltpu.VMEM((8, W * KPT, 128), F32),
            pltpu.VMEM((KPT, 256, 256), BF),
            pltpu.VMEM((KPT, W, 2 * W), BF),
            pltpu.VMEM((64, 1, 128), F32),
            pltpu.VMEM((8, 1, 128), F32),
            dma, dma, dma, dma((2,)), dma((2,)), dma((2,)), dma((2,)), dma, dma, dma, dma((2,)), dma, dma((2,)),
        ],
        compiler_params=pltpu.CompilerParams(
            collective_id=0, has_side_effects=True, vmem_limit_bytes=56 * 1024 * 1024
        ),
        name="orbital",
    )(kgrid, rvec, degen.reshape(1, NR), operators, vectors)
    return density, magnet.reshape(3)


def solution(mesh):
    return jax.shard_map(
        per_device,
        mesh=mesh,
        in_specs=(P(None, ("ka", "op", "row")), P(), P(), P("op", ("ka", "row"), None), P(("ka", "op", "row"), None)),
        out_specs=(P(None, ("ka", "op", "row")), P()),
        check_vma=False,
    )
```

```python
import functools
import math

import jax
import jax.numpy as jnp
from jax import lax
from jax.experimental import pallas as pl
from jax.experimental.pallas import tpu as pltpu
from jax.sharding import PartitionSpec as P

W = 80
GRID = 64
SMEARING = 0.5
NX, NY, NZ, NC = 4, 8, 8, 2
XC = NX * NC
RING = 8
KPT = 8
NR = 256
HALF = W * W
CHUNK = 256
CHUNKS = HALF // CHUNK
FIRST_Q = 13
KPOINTS = 4096
TOGETHER = 2
MESH = pl.DeviceIdType.MESH
BF = jnp.bfloat16
F32 = jnp.float32


def place():
    ka = lax.axis_index("ka")
    return lax.axis_index("op"), lax.div(ka, 2), lax.rem(ka, 2), lax.axis_index("row")


def at(x, y, c, z):
    return (2 * y + c, x, z)


def held_p(c, z):
    live = (c == 0) | (lax.rem(z, 2) == 0) | (z == 7)
    return live, jnp.where(c == 0, z, 8 + lax.div(z + 1, 2))


def held_q(c, y):
    live = (c == 1) | (lax.rem(y, 2) == 0)
    return live, FIRST_Q + jnp.where(c == 1, y, 8 + lax.div(y, 2))


FAR = (4, 3, 5, 2, 6, 1, 7)


def settle(ref, sem):
    pltpu.make_async_copy(ref, ref, sem).wait()


def push(src, dst, send_sem, recv_sem, device):
    pltpu.make_async_remote_copy(
        src_ref=src, dst_ref=dst, send_sem=send_sem, recv_sem=recv_sem,
        device_id=device, device_id_type=MESH,
    ).start()


def keep(src, dst, sem):
    pltpu.make_async_copy(src, dst, sem).start()


def each(count, body):
    def step(i, carry):
        body(i)
        return carry

    lax.fori_loop(0, count, step, 0)


def around(place, step):
    return lax.rem(place + step, RING)


def partners(x, c):
    order = ((2, 0), (2, 1), (1, 0), (3, 0), (1, 1), (3, 1), (0, 1), (0, 0))
    found = []
    for dx, dc in order:
        px, pc = lax.rem(x + dx, NX), (1 - c if dc else c)
        found.append((px, pc, 2 * px + pc))
    return found


def iota(shape, dim):
    return lax.broadcasted_iota(jnp.int32, shape, dim)


def dot(a, b):
    return jnp.dot(a, b, preferred_element_type=F32)


def matrix_rows(tile, put):
    lane = iota((KPT, 128), 1)
    for i in range(W):
        first, off = divmod(i * W, 128)
        row = tile(first)
        if off:
            row = pltpu.roll(row, 128 - off, 1)
            if off + W > 128:
                nxt = pltpu.roll(tile(first + 1), 128 - off, 1)
                row = jnp.where(lane < 128 - off, row, nxt)
        put(i, jnp.where(lane < W, row, 0.0))


def fold_table(rows_ref, lattice, inverse, table):
    points = rows_ref[:, 0, :]
    spread = (lax.div(iota((512, 64), 0), 8) == iota((512, 64), 1)).astype(F32).astype(BF)
    wide = dot(spread, points.astype(BF))
    own = lax.rem(iota((512, 128), 0), 8) == lax.rem(iota((512, 128), 1), 8)
    wide = jnp.where(own, wide, 0.0).astype(BF)
    for part in range(4):
        winding = dot(wide[part * 128:(part + 1) * 128], lattice)
        winding = winding - GRID * jnp.floor(winding * (1.0 / GRID))
        upper = winding >= GRID // 2
        turn = jnp.where(upper, winding - (GRID // 2), winding) - (GRID // 4)
        sign = jnp.where(upper, -inverse, inverse)
        angle = turn * (2.0 * math.pi / GRID)
        sq = angle * angle
        odd = -1.0 / 39916800.0
        for term in (1.0 / 362880.0, -1.0 / 5040.0, 1.0 / 120.0, -1.0 / 6.0, 1.0):
            odd = odd * sq + term
        even = 1.0 / 479001600.0
        for term in (-1.0 / 3628800.0, 1.0 / 40320.0, -1.0 / 720.0, 1.0 / 24.0, -0.5, 1.0):
            even = even * sq + term
        table[part * 128:(part + 1) * 128, :NR] = (-odd * angle * sign).astype(BF)
        table[part * 128:(part + 1) * 128, NR:] = (even * sign).astype(BF)


def transform(table, gathered, out):
    for part in range(4):
        rows = slice(part * 128, (part + 1) * 128)
        block = gathered[...].reshape(NR, 2 * CHUNK)
        turned = jnp.concatenate([-block[:, CHUNK:], block[:, :CHUNK]], axis=1)
        total = dot(table[rows, :NR], block) + dot(table[rows, NR:], turned)
        out[part * 16:(part + 1) * 16] = total.reshape(16, KPT, 2 * CHUNK).astype(BF)


def body(
    kgrid_hbm, rvec_hbm, degen_hbm, operators_hbm, vectors, density, magnet,
    kgrid, rvec, degen, operators, vec, own_row, k_p, k_q, in_p, in_q, stage, all_p, all_q, tab_p, tab_q,
    out_p, out_q, full, mats, right, left, sums, sums2,
    send1, send2, send3, k1_sem, k2_sem, in_sem, all_sem, full_sem, vec_sem, sum_send, sum_sem, kg_sem, small_sem, op_sem,
):
    x, y, c, z = place()
    xc = 2 * x + c
    live_p, chunk_p = held_p(c, z)
    live_q, chunk_q = held_q(c, y)
    barrier = pltpu.get_barrier_semaphore()
    keep(kgrid_hbm, kgrid, kg_sem)
    keep(rvec_hbm, rvec, small_sem.at[0])
    keep(degen_hbm, degen, small_sem.at[1])
    keep(operators_hbm, operators, op_sem)
    keep(vectors, vec, vec_sem)
    columns = partners(x, c)

    for px, pc, _ in columns[:-1]:
        pl.semaphore_signal(barrier, inc=1, device_id=at(px, y, pc, z), device_id_type=MESH)
    for step in FAR:
        for pc in (c, 1 - c):
            pl.semaphore_signal(barrier, inc=1, device_id=at(x, y, pc, around(z, step)), device_id_type=MESH)
            pl.semaphore_signal(barrier, inc=1, device_id=at(x, around(y, step), pc, z), device_id_type=MESH)
    pltpu.make_async_copy(kgrid_hbm, kgrid, kg_sem).wait()

    stage[...] = jnp.zeros_like(stage)
    stage[0:3, 0:KPT] = kgrid[...].astype(F32)
    row = stage[0:1, 0:128]
    row = row + pltpu.roll(stage[1:2, 0:128], 8, 1) + pltpu.roll(stage[2:3, 0:128], 16, 1)
    own_row[0] = row
    k_p[xc * 8 + z] = row
    k_q[xc * 8 + y] = row

    pltpu.make_async_copy(operators_hbm, operators, op_sem).wait()
    pl.semaphore_wait(barrier, 7 + 14 + 14)

    for step in FAR:
        push(own_row.at[0], k_p.at[xc * 8 + z], send1, k1_sem.at[0], at(x, y, c, around(z, step)))
        push(own_row.at[0], k_q.at[xc * 8 + y], send1, k1_sem.at[1], at(x, around(y, step), c, z))

    def pieces(chunk, dst, sem, device, local):
        for part in range(2):
            col = pl.multiple_of(part * HALF + chunk * CHUNK, 128)
            src = operators.at[0, :, pl.ds(col, CHUNK)]
            if local:
                keep(src, dst.at[part], sem)
            else:
                push(src, dst.at[part], send2, sem, device)

    def offer(step, pc):
        ring = around(z, step)
        live, chunk = held_p(pc, ring)

        @pl.when(live)
        def _():
            pieces(chunk, in_p.at[c * 8 + z], in_sem.at[0], at(x, y, pc, ring), False)

        ring2 = around(y, step)
        live2, chunk2 = held_q(pc, ring2)

        @pl.when(live2)
        def _():
            pieces(chunk2, in_q.at[c * 8 + y], in_sem.at[1], at(x, ring2, pc, z), False)

    for step in FAR:
        offer(step, c)
        offer(step, 1 - c)
    offer(0, 1 - c)

    @pl.when(live_p)
    def _():
        pieces(chunk_p, in_p.at[c * 8 + z], in_sem.at[0], None, True)

    @pl.when(live_q)
    def _():
        pieces(chunk_q, in_q.at[c * 8 + y], in_sem.at[1], None, True)

    settle(k_p.at[pl.ds(0, 7)], k1_sem.at[0])
    settle(k_q.at[pl.ds(0, 7)], k1_sem.at[1])

    for px, pc, _ in columns[:-1]:
        push(k_p.at[pl.ds(xc * 8, 8)], k_p.at[pl.ds(xc * 8, 8)], send1, k2_sem.at[0], at(px, y, pc, z))
        push(k_q.at[pl.ds(xc * 8, 8)], k_q.at[pl.ds(xc * 8, 8)], send1, k2_sem.at[1], at(px, y, pc, z))

    def collect(incoming, gathered, slot, sem, gather_sem, along_y):
        settle(incoming, sem)
        for s in range(16):
            for part in range(2):
                stage[2 * s:2 * s + 2, part * CHUNK:(part + 1) * CHUNK] = incoming[s, part].astype(F32)
        gathered[slot] = stage[...].astype(BF)

        for step in FAR:
            device = at(x, around(y, step), c, z) if along_y else at(x, y, c, around(z, step))
            push(gathered.at[slot], gathered.at[slot], send3, gather_sem, device)

    @pl.when(live_p)
    def _():
        collect(in_p, all_p, y, in_sem.at[0], all_sem.at[0], True)

    @pl.when(live_q)
    def _():
        collect(in_q, all_q, z, in_sem.at[1], all_sem.at[1], False)

    pltpu.make_async_copy(vectors, vec, vec_sem).wait()
    for part in range(2):
        def put(i, val, part=part):
            mats[part, i * KPT:(i + 1) * KPT, :] = val

        matrix_rows(lambda t, part=part: vec[:, part * HALF + t * 128: part * HALF + (t + 1) * 128].astype(F32), put)

    lane = iota((W, 128), 1)

    def eigen(k):
        vr = mats[0, pl.ds(k, W, stride=KPT), :]
        vi = mats[1, pl.ds(k, W, stride=KPT), :]
        gap = jnp.zeros((48, 256), BF)
        right[k, 0:W, :] = jnp.concatenate([vr, vi], axis=1).astype(BF)
        right[k, W:128, :] = gap
        right[k, 128:128 + W, :] = jnp.concatenate([-vi, vr], axis=1).astype(BF)
        right[k, 128 + W:, :] = gap
        fill = jnp.zeros((48, 128), F32)
        tr = jnp.transpose(jnp.concatenate([vr, fill], axis=0))[:W]
        ti = jnp.transpose(jnp.concatenate([vi, fill], axis=0))[:W]
        left[k] = paired(tr, ti).astype(BF)

    def paired(re, im):
        moved = pltpu.roll(im, W, 1)
        return jnp.concatenate([jnp.where(lane < W, re, moved), moved[:, :2 * W - 128]], axis=1)

    each(KPT, eigen)

    pltpu.make_async_copy(rvec_hbm, rvec, small_sem.at[0]).wait()
    pltpu.make_async_copy(degen_hbm, degen, small_sem.at[1]).wait()
    settle(k_p.at[pl.ds(0, 56)], k2_sem.at[0])
    settle(k_q.at[pl.ds(0, 56)], k2_sem.at[1])
    lattice_rows = iota((128, NR), 0)
    rv = rvec[...].astype(F32)
    lattice = jnp.where(
        lattice_rows < 8, rv[0:1],
        jnp.where(lattice_rows < 16, rv[1:2], jnp.where(lattice_rows < 24, rv[2:3], 0.0)),
    )
    weight = degen[...].astype(F32)

    @pl.when(live_p)
    def _():
        fold_table(k_p, lattice.astype(BF), 1.0 / weight, tab_p)

    @pl.when(live_q)
    def _():
        col = iota((NR, NR), 1)
        source = (
            lax.rem(lax.div(col, 2), 8) * 32 + lax.rem(lax.div(col, 16), 2) * 16
            + lax.div(col, 32) * 2 + lax.rem(col, 2)
        )
        swap = (iota((NR, NR), 0) == source).astype(F32).astype(BF)
        moved = dot(lattice.astype(BF), swap).astype(BF)
        weights = dot(jnp.broadcast_to(weight, (8, NR)).astype(BF), swap)[0:1]
        fold_table(k_q, moved, 1.0 / weights, tab_q)

    def deliver(chunk, out, along_z):
        dst = full.at[x, chunk]

        def one(step, some):
            ring = around(z if along_z else y, step)
            for px, pc, pxc in some:
                device = at(px, y, pc, ring) if along_z else at(px, ring, pc, z)
                push(out.at[pxc * 8 + ring], dst, send3, full_sem, device)

        def far(i):
            half = lax.div(i + 1, 2)
            one(jnp.where(lax.rem(i, 2) == 0, 4 + half, 4 - half), columns)

        each(7, far)
        one(0, columns[:-1])
        keep(out.at[xc * 8 + (z if along_z else y)], dst, full_sem)

    @pl.when(live_p)
    def _():
        settle(all_p.at[pl.ds(0, 7)], all_sem.at[0])
        transform(tab_p, all_p, out_p)
        deliver(chunk_p, out_p, True)

    @pl.when(live_q)
    def _():
        settle(all_q.at[pl.ds(0, 7)], all_sem.at[1])
        transform(tab_q, all_q, out_q)
        deliver(chunk_q, out_q, False)

    settle(full, full_sem)

    def rebuild(o):
        for part in range(2):
            def put(i, val, part=part):
                mats[2 * o + part, i * KPT:(i + 1) * KPT, :] = val

            matrix_rows(
                lambda t, part=part: full[o, t // 2, :, part * CHUNK + (t % 2) * 128: part * CHUNK + (t % 2 + 1) * 128].astype(F32),
                put,
            )

    each(4, rebuild)

    sub = iota((W, 128), 0)
    density_lane = iota((1, 128), 1)

    def point(k, carry):
        ops = [
            jnp.concatenate(
                [mats[2 * o, pl.ds(k, W, stride=KPT), :], mats[2 * o + 1, pl.ds(k, W, stride=KPT), :]], axis=1
            ).astype(BF)
            for o in range(4)
        ]
        prod = dot(jnp.concatenate(ops, axis=0), right[k])
        turn = left[k]
        rot = []
        for o in range(4):
            re = prod[o * W:(o + 1) * W, :128]
            im = prod[o * W:(o + 1) * W, 128:]
            stacked = jnp.concatenate(
                [jnp.concatenate([re, im], axis=1), jnp.concatenate([im, -re], axis=1)],
                axis=0,
            ).astype(BF)
            rot.append(dot(turn, stacked).astype(BF).astype(F32))
        ham_re, ham_im = rot[0][:, :128], rot[0][:, 128:]
        diag = jnp.where(sub == lane, ham_re, 0.0)
        down = 1.0 / (1.0 + jnp.exp(jnp.sum(diag, axis=1, keepdims=True) * (1.0 / SMEARING)))
        along = 1.0 / (1.0 + jnp.exp(jnp.sum(diag, axis=0, keepdims=True) * (1.0 / SMEARING)))
        weight2 = (1.0 - down) * along
        ham = paired(ham_re, ham_im).astype(BF)
        prods, turned = [], []
        fill = jnp.zeros((48, 128), F32)
        for b in range(3):
            re, im = rot[b + 1][:, :128], rot[b + 1][:, 128:]
            stacked = jnp.concatenate(
                [jnp.concatenate([re, im], axis=1), jnp.concatenate([-im, re], axis=1)],
                axis=0,
            ).astype(BF)
            prods.append(dot(ham, stacked))
            turned.append((
                jnp.transpose(jnp.concatenate([re, fill], axis=0))[:W] * weight2,
                jnp.transpose(jnp.concatenate([im, fill], axis=0))[:W] * weight2,
            ))
        for comp, (a, b) in enumerate(((1, 2), (2, 0), (0, 1))):
            terms = (
                turned[a][0] * prods[b][:, 128:] + turned[a][1] * prods[b][:, :128]
                - turned[b][0] * prods[a][:, 128:] - turned[b][1] * prods[a][:, :128]
            )
            total = jnp.sum(jnp.sum(terms, axis=0, keepdims=True), axis=1, keepdims=True) * (1.0 / W)
            stage[comp:comp + 1, 0:128] = stage[comp:comp + 1, 0:128] + jnp.where(density_lane == k, total, 0.0)
        return carry

    stage[0:8, 0:128] = jnp.zeros((8, 128), F32)
    def points(i, carry):
        for j in range(TOGETHER):
            carry = point(TOGETHER * i + j, carry)
        return carry

    lax.fori_loop(0, KPT // TOGETHER, points, 0)
    dens = stage[0:8, 0:128]
    density[...] = dens[0:3, 0:KPT]

    total = jnp.sum(dens, axis=1, keepdims=True)
    eye = iota((8, 128), 0) == iota((8, 128), 1)
    part = jnp.sum(jnp.where(eye, total, 0.0), axis=0, keepdims=True)
    sums[xc * 8 + z] = part

    def tell(step, some):
        ring = around(z, step)
        for px, pc, _ in some:
            push(sums.at[xc * 8 + z], sums.at[xc * 8 + z], sum_send, sum_sem.at[0], at(px, y, pc, ring))

    def tell_far(i):
        half = lax.div(i + 1, 2)
        tell(jnp.where(lax.rem(i, 2) == 0, 4 + half, 4 - half), columns)

    each(7, tell_far)
    tell(0, columns[:-1])
    settle(sums.at[pl.ds(0, 63)], sum_sem.at[0])
    sums2[y] = jnp.sum(sums[:, 0, :], axis=0, keepdims=True)
    for step in FAR:
        push(sums2.at[y], sums2.at[y], sum_send, sum_sem.at[1], at(x, around(y, step), c, z))
    settle(sums2.at[pl.ds(0, 7)], sum_sem.at[1])
    part = jnp.sum(sums2[:, 0, :], axis=0, keepdims=True)
    magnet[...] = part[:, 0:3] * (1.0 / KPOINTS)

    settle(sums.at[pl.ds(0, 63)], sum_send)
    settle(sums2.at[pl.ds(0, 7)], sum_send)
    settle(k_p.at[pl.ds(0, 14)], send1)
    settle(k_p.at[pl.ds(0, 56)], send1)
    settle(k_p.at[pl.ds(0, 56)], send1)

    settle(in_p.at[pl.ds(0, 12)], send2)

    @pl.when(jnp.logical_not(live_p))
    def _():
        settle(in_p.at[pl.ds(0, 1)], send2)

    settle(in_q.at[pl.ds(0, 11)], send2)

    @pl.when(jnp.logical_not(live_q))
    def _():
        settle(in_q.at[pl.ds(0, 1)], send2)

    @pl.when(live_p)
    def _():
        settle(all_p.at[pl.ds(0, 7)], send3)
        settle(out_p.at[pl.ds(0, 63)], send3)

    @pl.when(live_q)
    def _():
        settle(all_q.at[pl.ds(0, 7)], send3)
        settle(out_q.at[pl.ds(0, 63)], send3)


def per_device(kgrid, rvec, degen, operators, vectors):
    vmem = pl.BlockSpec(memory_space=pltpu.VMEM)
    anywhere = pl.BlockSpec(memory_space=pl.ANY)
    dma = pltpu.SemaphoreType.DMA
    density, magnet = pl.pallas_call(
        body,
        out_shape=(jax.ShapeDtypeStruct((3, KPT), F32), jax.ShapeDtypeStruct((1, 3), F32)),
        in_specs=[anywhere] * 5,
        out_specs=(vmem, vmem),
        scratch_shapes=[
            pltpu.VMEM((3, KPT), jnp.int32),
            pltpu.VMEM((3, NR), jnp.int32),
            pltpu.VMEM((1, NR), jnp.int32),
            pltpu.VMEM((1, 2, 2 * HALF), BF),
            pltpu.VMEM((KPT, 2 * HALF), BF),
            pltpu.VMEM((1, 1, 128), F32),
            pltpu.VMEM((64, 1, 128), F32),
            pltpu.VMEM((64, 1, 128), F32),
            pltpu.VMEM((16, 2, 2, CHUNK), BF),
            pltpu.VMEM((16, 2, 2, CHUNK), BF),
            pltpu.VMEM((32, 2 * CHUNK), F32),
            pltpu.VMEM((RING, 32, 2 * CHUNK), BF),
            pltpu.VMEM((RING, 32, 2 * CHUNK), BF),
            pltpu.VMEM((512, 2 * NR), BF),
            pltpu.VMEM((512, 2 * NR), BF),
            pltpu.VMEM((64, KPT, 2 * CHUNK), BF),
            pltpu.VMEM((64, KPT, 2 * CHUNK), BF),
            pltpu.VMEM((4, CHUNKS, KPT, 2 * CHUNK), BF),
            pltpu.VMEM((8, W * KPT, 128), F32),
            pltpu.VMEM((KPT, 256, 256), BF),
            pltpu.VMEM((KPT, W, 2 * W), BF),
            pltpu.VMEM((64, 1, 128), F32),
            pltpu.VMEM((8, 1, 128), F32),
            dma, dma, dma, dma((2,)), dma((2,)), dma((2,)), dma((2,)), dma, dma, dma, dma((2,)), dma, dma((2,)), dma,
        ],
        compiler_params=pltpu.CompilerParams(
            collective_id=0, has_side_effects=True, vmem_limit_bytes=56 * 1024 * 1024
        ),
        name="orbital",
    )(kgrid, rvec, degen.reshape(1, NR), operators, vectors)
    return density, magnet.reshape(3)


def solution(mesh):
    return jax.shard_map(
        per_device,
        mesh=mesh,
        in_specs=(P(None, ("ka", "op", "row")), P(), P(), P("op", ("ka", "row"), None), P(("ka", "op", "row"), None)),
        out_specs=(P(None, ("ka", "op", "row")), P()),
        check_vma=False,
    )
```

```python
import functools
import math

import jax
import jax.numpy as jnp
from jax import lax
from jax.experimental import pallas as pl
from jax.experimental.pallas import tpu as pltpu
from jax.sharding import PartitionSpec as P

W = 80
GRID = 64
SMEARING = 0.5
NX, NY, NZ, NC = 4, 8, 8, 2
XC = NX * NC
RING = 8
KPT = 8
NR = 256
HALF = W * W
CHUNK = 256
CHUNKS = HALF // CHUNK
FIRST_Q = 13
KPOINTS = 4096
MESH = pl.DeviceIdType.MESH
BF = jnp.bfloat16
F32 = jnp.float32


def place():
    ka = lax.axis_index("ka")
    return lax.axis_index("op"), lax.div(ka, 2), lax.rem(ka, 2), lax.axis_index("row")


def at(x, y, c, z):
    return (2 * y + c, x, z)


def held_p(c, z):
    live = (c == 0) | (lax.rem(z, 2) == 0) | (z == 7)
    return live, jnp.where(c == 0, z, 8 + lax.div(z + 1, 2))


def held_q(c, y):
    live = (c == 1) | (lax.rem(y, 2) == 0)
    return live, FIRST_Q + jnp.where(c == 1, y, 8 + lax.div(y, 2))


FAR = (4, 3, 5, 2, 6, 1, 7)


def settle(ref, sem):
    pltpu.make_async_copy(ref, ref, sem).wait()


def push(src, dst, send_sem, recv_sem, device):
    pltpu.make_async_remote_copy(
        src_ref=src, dst_ref=dst, send_sem=send_sem, recv_sem=recv_sem,
        device_id=device, device_id_type=MESH,
    ).start()


def keep(src, dst, sem):
    pltpu.make_async_copy(src, dst, sem).start()


def each(count, body):
    def step(i, carry):
        body(i)
        return carry

    lax.fori_loop(0, count, step, 0)


def around(place, step):
    return lax.rem(place + step, RING)


def partners(x, c):
    order = ((2, 0), (2, 1), (1, 0), (3, 0), (1, 1), (3, 1), (0, 1), (0, 0))
    found = []
    for dx, dc in order:
        px, pc = lax.rem(x + dx, NX), (1 - c if dc else c)
        found.append((px, pc, 2 * px + pc))
    return found


def iota(shape, dim):
    return lax.broadcasted_iota(jnp.int32, shape, dim)


def dot(a, b):
    return jnp.dot(a, b, preferred_element_type=F32)


def matrix_rows(tile, put):
    lane = iota((KPT, 128), 1)
    for i in range(W):
        first, off = divmod(i * W, 128)
        row = tile(first)
        if off:
            row = pltpu.roll(row, 128 - off, 1)
            if off + W > 128:
                nxt = pltpu.roll(tile(first + 1), 128 - off, 1)
                row = jnp.where(lane < 128 - off, row, nxt)
        put(i, jnp.where(lane < W, row, 0.0))


def fold_table(rows_ref, lattice, inverse, table):
    points = rows_ref[:, 0, :]
    spread = (lax.div(iota((512, 64), 0), 8) == iota((512, 64), 1)).astype(F32).astype(BF)
    wide = dot(spread, points.astype(BF))
    shift = (lax.div(lax.rem(iota((128, NR), 0), 8), 4) * (GRID // 4)).astype(F32)
    for block in range(8):
        half, rows = block // 4, slice((block % 4) * 128, (block % 4 + 1) * 128)
        own = half * 4 + lax.rem(iota((128, 128), 0), 4) == lax.rem(iota((128, 128), 1), 8)
        winding = dot(jnp.where(own, wide[rows], 0.0).astype(BF), lattice) - shift
        winding = winding - GRID * jnp.floor(winding * (1.0 / GRID))
        upper = winding >= GRID // 2
        turn = jnp.where(upper, winding - (GRID // 2), winding) - (GRID // 4)
        sign = jnp.where(upper, inverse, -inverse)
        angle = turn * (2.0 * math.pi / GRID)
        sq = angle * angle
        odd = -1.0 / 39916800.0
        for term in (1.0 / 362880.0, -1.0 / 5040.0, 1.0 / 120.0, -1.0 / 6.0, 1.0):
            odd = odd * sq + term
        even = 1.0 / 479001600.0
        for term in (-1.0 / 3628800.0, 1.0 / 40320.0, -1.0 / 720.0, 1.0 / 24.0, -0.5, 1.0):
            even = even * sq + term
        table[block * 128:(block + 1) * 128, :NR] = (odd * angle * sign).astype(BF)
        table[block * 128:(block + 1) * 128, NR:] = (even * sign).astype(BF)


def transform(table, gathered, out, half):
    for part in range(2):
        rows = slice(half * 512 + part * 256, half * 512 + (part + 1) * 256)
        block = gathered[...].reshape(NR, 2 * CHUNK)
        total = dot(table[rows, :NR], block[:, :CHUNK]) + dot(table[rows, NR:], block[:, CHUNK:])
        out[half, part * 32:(part + 1) * 32] = total.reshape(32, KPT, CHUNK).astype(BF)


def body(
    kgrid_hbm, rvec_hbm, degen_hbm, operators_hbm, vectors, density, magnet,
    kgrid, rvec, degen, operators, vec, own_row, k_p, k_q, in_p, in_q, stage, all_p, all_q, tab_p, tab_q,
    out_p, out_q, full, mats, right, left, sums, sums2,
    send1, send2, send3, k1_sem, k2_sem, in_sem, all_sem, full_sem, vec_sem, sum_send, sum_sem, kg_sem, small_sem, op_sem,
):
    x, y, c, z = place()
    xc = 2 * x + c
    live_p, chunk_p = held_p(c, z)
    live_q, chunk_q = held_q(c, y)
    barrier = pltpu.get_barrier_semaphore()
    keep(kgrid_hbm, kgrid, kg_sem)
    keep(rvec_hbm, rvec, small_sem.at[0])
    keep(degen_hbm, degen, small_sem.at[1])
    keep(operators_hbm, operators, op_sem)
    keep(vectors, vec, vec_sem)
    columns = partners(x, c)

    for px, pc, _ in columns[:-1]:
        pl.semaphore_signal(barrier, inc=1, device_id=at(px, y, pc, z), device_id_type=MESH)
    for step in FAR:
        for pc in (c, 1 - c):
            pl.semaphore_signal(barrier, inc=1, device_id=at(x, y, pc, around(z, step)), device_id_type=MESH)
            pl.semaphore_signal(barrier, inc=1, device_id=at(x, around(y, step), pc, z), device_id_type=MESH)
    pltpu.make_async_copy(kgrid_hbm, kgrid, kg_sem).wait()

    stage[...] = jnp.zeros_like(stage)
    stage[0:3, 0:KPT] = kgrid[...].astype(F32)
    row = stage[0:1, 0:128]
    row = row + pltpu.roll(stage[1:2, 0:128], 8, 1) + pltpu.roll(stage[2:3, 0:128], 16, 1)
    own_row[0] = row
    k_p[xc * 8 + z] = row
    k_q[xc * 8 + y] = row

    pltpu.make_async_copy(operators_hbm, operators, op_sem).wait()
    pl.semaphore_wait(barrier, 7 + 14 + 14)

    for step in FAR:
        push(own_row.at[0], k_p.at[xc * 8 + z], send1, k1_sem.at[0], at(x, y, c, around(z, step)))
        push(own_row.at[0], k_q.at[xc * 8 + y], send1, k1_sem.at[1], at(x, around(y, step), c, z))

    def pieces(chunk, dst, sem, device, local):
        for part in range(2):
            col = pl.multiple_of(part * HALF + chunk * CHUNK, 128)
            src = operators.at[0, :, pl.ds(col, CHUNK)]
            if local:
                keep(src, dst.at[part], sem)
            else:
                push(src, dst.at[part], send2, sem, device)

    def offer(step, pc):
        ring = around(z, step)
        live, chunk = held_p(pc, ring)

        @pl.when(live)
        def _():
            pieces(chunk, in_p.at[c * 8 + z], in_sem.at[0], at(x, y, pc, ring), False)

        ring2 = around(y, step)
        live2, chunk2 = held_q(pc, ring2)

        @pl.when(live2)
        def _():
            pieces(chunk2, in_q.at[c * 8 + y], in_sem.at[1], at(x, ring2, pc, z), False)

    for step in FAR:
        offer(step, c)
        offer(step, 1 - c)
    offer(0, 1 - c)

    @pl.when(live_p)
    def _():
        pieces(chunk_p, in_p.at[c * 8 + z], in_sem.at[0], None, True)

    @pl.when(live_q)
    def _():
        pieces(chunk_q, in_q.at[c * 8 + y], in_sem.at[1], None, True)

    settle(k_p.at[pl.ds(0, 7)], k1_sem.at[0])
    settle(k_q.at[pl.ds(0, 7)], k1_sem.at[1])

    for px, pc, _ in columns[:-1]:
        push(k_p.at[pl.ds(xc * 8, 8)], k_p.at[pl.ds(xc * 8, 8)], send1, k2_sem.at[0], at(px, y, pc, z))
        push(k_q.at[pl.ds(xc * 8, 8)], k_q.at[pl.ds(xc * 8, 8)], send1, k2_sem.at[1], at(px, y, pc, z))

    def collect(incoming, gathered, slot, sem, gather_sem, along_y):
        settle(incoming, sem)
        for s in range(16):
            for part in range(2):
                stage[2 * s:2 * s + 2, part * CHUNK:(part + 1) * CHUNK] = incoming[s, part].astype(F32)
        gathered[slot] = stage[...].astype(BF)

        for step in FAR:
            device = at(x, around(y, step), c, z) if along_y else at(x, y, c, around(z, step))
            push(gathered.at[slot], gathered.at[slot], send3, gather_sem, device)

    @pl.when(live_p)
    def _():
        collect(in_p, all_p, y, in_sem.at[0], all_sem.at[0], True)

    @pl.when(live_q)
    def _():
        collect(in_q, all_q, z, in_sem.at[1], all_sem.at[1], False)

    pltpu.make_async_copy(vectors, vec, vec_sem).wait()
    for part in range(2):
        def put(i, val, part=part):
            mats[part, i * KPT:(i + 1) * KPT, :] = val

        matrix_rows(lambda t, part=part: vec[:, part * HALF + t * 128: part * HALF + (t + 1) * 128].astype(F32), put)

    lane = iota((W, 128), 1)

    def eigen(k):
        vr = mats[0, pl.ds(k, W, stride=KPT), :]
        vi = mats[1, pl.ds(k, W, stride=KPT), :]
        gap = jnp.zeros((48, 256), BF)
        right[k, 0:W, :] = jnp.concatenate([vr, vi], axis=1).astype(BF)
        right[k, W:128, :] = gap
        right[k, 128:128 + W, :] = jnp.concatenate([-vi, vr], axis=1).astype(BF)
        right[k, 128 + W:, :] = gap
        fill = jnp.zeros((48, 128), F32)
        tr = jnp.transpose(jnp.concatenate([vr, fill], axis=0))[:W]
        ti = jnp.transpose(jnp.concatenate([vi, fill], axis=0))[:W]
        left[k] = paired(tr, ti).astype(BF)

    def paired(re, im):
        moved = pltpu.roll(im, W, 1)
        return jnp.concatenate([jnp.where(lane < W, re, moved), moved[:, :2 * W - 128]], axis=1)

    each(KPT, eigen)

    pltpu.make_async_copy(rvec_hbm, rvec, small_sem.at[0]).wait()
    pltpu.make_async_copy(degen_hbm, degen, small_sem.at[1]).wait()
    settle(k_p.at[pl.ds(0, 56)], k2_sem.at[0])
    settle(k_q.at[pl.ds(0, 56)], k2_sem.at[1])
    lattice_rows = iota((128, NR), 0)
    rv = rvec[...].astype(F32)
    lattice = jnp.where(
        lattice_rows < 8, rv[0:1],
        jnp.where(lattice_rows < 16, rv[1:2], jnp.where(lattice_rows < 24, rv[2:3], 0.0)),
    )
    weight = degen[...].astype(F32)

    @pl.when(live_p)
    def _():
        fold_table(k_p, lattice.astype(BF), 1.0 / weight, tab_p)

    @pl.when(live_q)
    def _():
        col = iota((NR, NR), 1)
        source = (
            lax.rem(lax.div(col, 2), 8) * 32 + lax.rem(lax.div(col, 16), 2) * 16
            + lax.div(col, 32) * 2 + lax.rem(col, 2)
        )
        swap = (iota((NR, NR), 0) == source).astype(F32).astype(BF)
        moved = dot(lattice.astype(BF), swap).astype(BF)
        weights = dot(jnp.broadcast_to(weight, (8, NR)).astype(BF), swap)[0:1]
        fold_table(k_q, moved, 1.0 / weights, tab_q)

    def deliver(chunk, out, along_z, half):
        dst = full.at[half, x, chunk]

        def one(step, some):
            ring = around(z if along_z else y, step)
            for px, pc, pxc in some:
                device = at(px, y, pc, ring) if along_z else at(px, ring, pc, z)
                push(out.at[half, pxc * 8 + ring], dst, send3, full_sem.at[half], device)

        def far(i):
            half = lax.div(i + 1, 2)
            one(jnp.where(lax.rem(i, 2) == 0, 4 + half, 4 - half), columns)

        each(7, far)
        one(0, columns[:-1])
        keep(out.at[half, xc * 8 + (z if along_z else y)], dst, full_sem.at[half])

    @pl.when(live_p)
    def _():
        settle(all_p.at[pl.ds(0, 7)], all_sem.at[0])
        transform(tab_p, all_p, out_p, 0)
        deliver(chunk_p, out_p, True, 0)

    @pl.when(live_q)
    def _():
        settle(all_q.at[pl.ds(0, 7)], all_sem.at[1])
        transform(tab_q, all_q, out_q, 0)
        deliver(chunk_q, out_q, False, 0)

    @pl.when(live_p)
    def _():
        transform(tab_p, all_p, out_p, 1)
        deliver(chunk_p, out_p, True, 1)

    @pl.when(live_q)
    def _():
        transform(tab_q, all_q, out_q, 1)
        deliver(chunk_q, out_q, False, 1)

    sub = iota((W, 128), 0)

    def rotate(half):
        settle(full.at[half], full_sem.at[half])

        def rebuild(o):
            def put(i, val):
                mats[o, i * KPT:(i + 1) * KPT, :] = val

            matrix_rows(lambda t: full[half, o, t // 2, :, (t % 2) * 128:(t % 2 + 1) * 128].astype(F32), put)

        each(4, rebuild)
        group = range(4)
        prods = []
        for k in group:
            ops = [
                jnp.concatenate(
                    [mats[o, pl.ds(k, W, stride=KPT), :], mats[o, pl.ds(4 + k, W, stride=KPT), :]], axis=1
                ).astype(BF)
                for o in range(4)
            ]
            prods.append(dot(jnp.concatenate(ops, axis=0), right[half * 4 + k]).astype(BF))
        rots = [[] for _ in group]
        for o in range(4):
            for k in group:
                re = prods[k][o * W:(o + 1) * W, :128]
                im = prods[k][o * W:(o + 1) * W, 128:]
                stacked = jnp.concatenate(
                    [jnp.concatenate([re, im], axis=1), jnp.concatenate([im, -re], axis=1)], axis=0
                )
                rots[k].append(dot(left[half * 4 + k], stacked).astype(BF))
        hams, weights = [], []
        for k in group:
            ham_re, ham_im = rots[k][0][:, :128].astype(F32), rots[k][0][:, 128:].astype(F32)
            diag = jnp.where(sub == lane, ham_re, 0.0)
            down = 1.0 / (1.0 + jnp.exp(jnp.sum(diag, axis=1, keepdims=True) * (1.0 / SMEARING)))
            along = 1.0 / (1.0 + jnp.exp(jnp.sum(diag, axis=0, keepdims=True) * (1.0 / SMEARING)))
            weights.append((1.0 - down) * along)
            hams.append(paired(ham_re, ham_im).astype(BF))
        products = [[] for _ in group]
        turned = [[] for _ in group]
        fill = jnp.zeros((48, 128), F32)
        for b in range(3):
            for k in group:
                re, im = rots[k][b + 1][:, :128], rots[k][b + 1][:, 128:]
                stacked = jnp.concatenate(
                    [jnp.concatenate([re, im], axis=1), jnp.concatenate([-im, re], axis=1)], axis=0
                )
                products[k].append(dot(hams[k], stacked))
                turned[k].append((
                    jnp.transpose(jnp.concatenate([re.astype(F32), fill], axis=0))[:W],
                    jnp.transpose(jnp.concatenate([im.astype(F32), fill], axis=0))[:W],
                ))
        spot8 = iota((KPT, 128), 0)
        for comp, (a, b) in enumerate(((1, 2), (2, 0), (0, 1))):
            found = jnp.zeros((KPT, 128), F32)
            for k in group:
                terms = (
                    turned[k][a][0] * products[k][b][:, 128:] + turned[k][a][1] * products[k][b][:, :128]
                    - turned[k][b][0] * products[k][a][:, 128:] - turned[k][b][1] * products[k][a][:, :128]
                ) * weights[k]
                found = jnp.where(spot8 == half * 4 + k, jnp.sum(terms, axis=0, keepdims=True) * (1.0 / W), found)
            stage[comp * KPT:(comp + 1) * KPT, 0:128] = stage[comp * KPT:(comp + 1) * KPT, 0:128] + found

    stage[...] = jnp.zeros_like(stage)
    each(2, rotate)
    spot = iota((1, 128), 1)
    part = jnp.zeros((1, 128), F32)
    for comp in range(3):
        sumk = jnp.sum(stage[comp * KPT:(comp + 1) * KPT, 0:128], axis=0, keepdims=True)
        part = part + jnp.where(spot == comp, jnp.sum(sumk, axis=1, keepdims=True), 0.0)

    sums[xc * 8 + z] = part

    def tell(step, some):
        ring = around(z, step)
        for px, pc, _ in some:
            push(sums.at[xc * 8 + z], sums.at[xc * 8 + z], sum_send, sum_sem.at[0], at(px, y, pc, ring))

    def tell_far(i):
        half = lax.div(i + 1, 2)
        tell(jnp.where(lax.rem(i, 2) == 0, 4 + half, 4 - half), columns)

    each(7, tell_far)
    tell(0, columns[:-1])
    eye = iota((KPT, 128), 0) == iota((KPT, 128), 1)
    for comp in range(3):
        column = jnp.sum(stage[comp * KPT:(comp + 1) * KPT, 0:128], axis=1, keepdims=True)
        density[comp:comp + 1] = jnp.sum(jnp.where(eye, column, 0.0), axis=0, keepdims=True)[:, 0:KPT]
    settle(sums.at[pl.ds(0, 63)], sum_sem.at[0])
    sums2[y] = jnp.sum(sums[:, 0, :], axis=0, keepdims=True)
    for step in FAR:
        push(sums2.at[y], sums2.at[y], sum_send, sum_sem.at[1], at(x, around(y, step), c, z))
    settle(sums2.at[pl.ds(0, 7)], sum_sem.at[1])
    part = jnp.sum(sums2[:, 0, :], axis=0, keepdims=True)
    magnet[...] = part[:, 0:3] * (1.0 / KPOINTS)

    settle(sums.at[pl.ds(0, 63)], sum_send)
    settle(sums2.at[pl.ds(0, 7)], sum_send)
    settle(k_p.at[pl.ds(0, 14)], send1)
    settle(k_p.at[pl.ds(0, 56)], send1)
    settle(k_p.at[pl.ds(0, 56)], send1)

    settle(in_p.at[pl.ds(0, 12)], send2)

    @pl.when(jnp.logical_not(live_p))
    def _():
        settle(in_p.at[pl.ds(0, 1)], send2)

    settle(in_q.at[pl.ds(0, 11)], send2)

    @pl.when(jnp.logical_not(live_q))
    def _():
        settle(in_q.at[pl.ds(0, 1)], send2)

    @pl.when(live_p)
    def _():
        settle(all_p.at[pl.ds(0, 7)], send3)
        for half in range(2):
            settle(out_p.at[half, pl.ds(0, 63)], send3)

    @pl.when(live_q)
    def _():
        settle(all_q.at[pl.ds(0, 7)], send3)
        for half in range(2):
            settle(out_q.at[half, pl.ds(0, 63)], send3)


def per_device(kgrid, rvec, degen, operators, vectors):
    vmem = pl.BlockSpec(memory_space=pltpu.VMEM)
    anywhere = pl.BlockSpec(memory_space=pl.ANY)
    dma = pltpu.SemaphoreType.DMA
    density, magnet = pl.pallas_call(
        body,
        out_shape=(jax.ShapeDtypeStruct((3, KPT), F32), jax.ShapeDtypeStruct((1, 3), F32)),
        in_specs=[anywhere] * 5,
        out_specs=(vmem, vmem),
        scratch_shapes=[
            pltpu.VMEM((3, KPT), jnp.int32),
            pltpu.VMEM((3, NR), jnp.int32),
            pltpu.VMEM((1, NR), jnp.int32),
            pltpu.VMEM((1, 2, 2 * HALF), BF),
            pltpu.VMEM((KPT, 2 * HALF), BF),
            pltpu.VMEM((1, 1, 128), F32),
            pltpu.VMEM((64, 1, 128), F32),
            pltpu.VMEM((64, 1, 128), F32),
            pltpu.VMEM((16, 2, 2, CHUNK), BF),
            pltpu.VMEM((16, 2, 2, CHUNK), BF),
            pltpu.VMEM((32, 2 * CHUNK), F32),
            pltpu.VMEM((RING, 32, 2 * CHUNK), BF),
            pltpu.VMEM((RING, 32, 2 * CHUNK), BF),
            pltpu.VMEM((1024, 2 * NR), BF),
            pltpu.VMEM((1024, 2 * NR), BF),
            pltpu.VMEM((2, 64, KPT, CHUNK), BF),
            pltpu.VMEM((2, 64, KPT, CHUNK), BF),
            pltpu.VMEM((2, 4, CHUNKS, KPT, CHUNK), BF),
            pltpu.VMEM((4, W * KPT, 128), F32),
            pltpu.VMEM((KPT, 256, 256), BF),
            pltpu.VMEM((KPT, W, 2 * W), BF),
            pltpu.VMEM((64, 1, 128), F32),
            pltpu.VMEM((8, 1, 128), F32),
            dma, dma, dma, dma((2,)), dma((2,)), dma((2,)), dma((2,)), dma((2,)), dma, dma, dma((2,)), dma, dma((2,)), dma,
        ],
        compiler_params=pltpu.CompilerParams(
            collective_id=0, has_side_effects=True, vmem_limit_bytes=56 * 1024 * 1024
        ),
        name="orbital",
    )(kgrid, rvec, degen.reshape(1, NR), operators, vectors)
    return density, magnet.reshape(3)


def solution(mesh):
    return jax.shard_map(
        per_device,
        mesh=mesh,
        in_specs=(P(None, ("ka", "op", "row")), P(), P(), P("op", ("ka", "row"), None), P(("ka", "op", "row"), None)),
        out_specs=(P(None, ("ka", "op", "row")), P()),
        check_vma=False,
    )
```

```python
import functools
import math

import jax
import jax.numpy as jnp
from jax import lax
from jax.experimental import pallas as pl
from jax.experimental.pallas import tpu as pltpu
from jax.sharding import PartitionSpec as P

W = 80
GRID = 64
SMEARING = 0.5
NX, NY, NZ, NC = 4, 8, 8, 2
XC = NX * NC
RING = 8
KPT = 8
NR = 256
HALF = W * W
CHUNK = 256
CHUNKS = HALF // CHUNK
FIRST_Q = 13
KPOINTS = 4096
MESH = pl.DeviceIdType.MESH
BF = jnp.bfloat16
F32 = jnp.float32


def place():
    ka = lax.axis_index("ka")
    return lax.axis_index("op"), lax.div(ka, 2), lax.rem(ka, 2), lax.axis_index("row")


def at(x, y, c, z):
    return (2 * y + c, x, z)


def held_p(c, z):
    live = (c == 0) | (lax.rem(z, 2) == 0) | (z == 7)
    return live, jnp.where(c == 0, z, 8 + lax.div(z + 1, 2))


def held_q(c, y):
    live = (c == 1) | (lax.rem(y, 2) == 0)
    return live, FIRST_Q + jnp.where(c == 1, y, 8 + lax.div(y, 2))


FAR = (4, 3, 5, 2, 6, 1, 7)


def settle(ref, sem):
    pltpu.make_async_copy(ref, ref, sem).wait()


def push(src, dst, send_sem, recv_sem, device):
    pltpu.make_async_remote_copy(
        src_ref=src, dst_ref=dst, send_sem=send_sem, recv_sem=recv_sem,
        device_id=device, device_id_type=MESH,
    ).start()


def keep(src, dst, sem):
    pltpu.make_async_copy(src, dst, sem).start()


def each(count, body):
    def step(i, carry):
        body(i)
        return carry

    lax.fori_loop(0, count, step, 0)


def around(place, step):
    return lax.rem(place + step, RING)


def partners(x, c):
    order = ((2, 0), (2, 1), (1, 0), (3, 0), (1, 1), (3, 1), (0, 1), (0, 0))
    found = []
    for dx, dc in order:
        px, pc = lax.rem(x + dx, NX), (1 - c if dc else c)
        found.append((px, pc, 2 * px + pc))
    return found


def iota(shape, dim):
    return lax.broadcasted_iota(jnp.int32, shape, dim)


def dot(a, b):
    return jnp.dot(a, b, preferred_element_type=F32)


def matrix_rows(tile, put):
    lane = iota((KPT, 128), 1)
    for i in range(W):
        first, off = divmod(i * W, 128)
        row = tile(first)
        if off:
            row = pltpu.roll(row, 128 - off, 1)
            if off + W > 128:
                nxt = pltpu.roll(tile(first + 1), 128 - off, 1)
                row = jnp.where(lane < 128 - off, row, nxt)
        put(i, jnp.where(lane < W, row, 0.0))


def fold_table(rows_ref, lattice, inverse, table):
    points = rows_ref[:, 0, :]
    spread = (lax.div(iota((256, 64), 0), 4) == iota((256, 64), 1)).astype(F32).astype(BF)
    wide = dot(spread, points.astype(BF))
    first = lax.rem(iota((128, NR), 0), 8) < 4
    for block in range(4):
        half, rows = block // 2, slice((block % 2) * 128, (block % 2 + 1) * 128)
        own = half * 4 + lax.rem(iota((128, 128), 0), 4) == lax.rem(iota((128, 128), 1), 8)
        winding = dot(jnp.where(own, wide[rows], 0.0).astype(BF), lattice)
        winding = winding - GRID * jnp.floor(winding * (1.0 / GRID))
        upper = winding >= GRID // 2
        turn = jnp.where(upper, winding - (GRID // 2), winding) - (GRID // 4)
        sign = jnp.where(upper, inverse, -inverse)
        angle = turn * (2.0 * math.pi / GRID)
        sq = angle * angle
        odd = -1.0 / 39916800.0
        for term in (1.0 / 362880.0, -1.0 / 5040.0, 1.0 / 120.0, -1.0 / 6.0, 1.0):
            odd = odd * sq + term
        even = 1.0 / 479001600.0
        for term in (-1.0 / 3628800.0, 1.0 / 40320.0, -1.0 / 720.0, 1.0 / 24.0, -0.5, 1.0):
            even = even * sq + term
        cosine = odd * angle * sign
        minus = even * sign
        pairs = []
        for upper_part, lower_part in ((cosine, -minus), (minus, cosine)):
            swapped_low = swap4(lower_part)
            swapped_up = swap4(upper_part)
            even_slot = jnp.where(first, upper_part, swapped_low).reshape(16, 1, 8, NR)
            odd_slot = jnp.where(first, swapped_up, lower_part).reshape(16, 1, 8, NR)
            pairs.append(jnp.concatenate([even_slot, odd_slot], axis=1).reshape(256, NR))
        table[block * 256:(block + 1) * 256, :NR] = pairs[0].astype(BF)
        table[block * 256:(block + 1) * 256, NR:] = pairs[1].astype(BF)


def swap4(val):
    return pltpu.roll(val.reshape(16, 8, NR), 4, 1).reshape(128, NR)


def transform(table, gathered, out, half):
    for part in range(2):
        rows = slice(half * 512 + part * 256, half * 512 + (part + 1) * 256)
        block = gathered[...].reshape(NR, 2 * CHUNK)
        total = dot(table[rows, :NR], block[:, :CHUNK]) + dot(table[rows, NR:], block[:, CHUNK:])
        out[half, part * 32:(part + 1) * 32] = total.reshape(32, KPT, CHUNK).astype(BF)


def body(
    kgrid_hbm, rvec_hbm, degen_hbm, operators_hbm, vectors, density, magnet,
    kgrid, rvec, degen, operators, vec, own_row, k_p, k_q, in_p, in_q, stage, all_p, all_q, tab_p, tab_q,
    out_p, out_q, full, mats, right, left, sums, sums2,
    send1, send2, send3, k1_sem, k2_sem, in_sem, all_sem, full_sem, vec_sem, sum_send, sum_sem, kg_sem, small_sem, op_sem,
):
    x, y, c, z = place()
    xc = 2 * x + c
    live_p, chunk_p = held_p(c, z)
    live_q, chunk_q = held_q(c, y)
    barrier = pltpu.get_barrier_semaphore()
    keep(kgrid_hbm, kgrid, kg_sem)
    keep(rvec_hbm, rvec, small_sem.at[0])
    keep(degen_hbm, degen, small_sem.at[1])
    keep(operators_hbm, operators, op_sem)
    keep(vectors, vec, vec_sem)
    columns = partners(x, c)

    for px, pc, _ in columns[:-1]:
        pl.semaphore_signal(barrier, inc=1, device_id=at(px, y, pc, z), device_id_type=MESH)
    for step in FAR:
        for pc in (c, 1 - c):
            pl.semaphore_signal(barrier, inc=1, device_id=at(x, y, pc, around(z, step)), device_id_type=MESH)
            pl.semaphore_signal(barrier, inc=1, device_id=at(x, around(y, step), pc, z), device_id_type=MESH)
    pltpu.make_async_copy(kgrid_hbm, kgrid, kg_sem).wait()

    stage[...] = jnp.zeros_like(stage)
    stage[0:3, 0:KPT] = kgrid[...].astype(F32)
    row = stage[0:1, 0:128]
    row = row + pltpu.roll(stage[1:2, 0:128], 8, 1) + pltpu.roll(stage[2:3, 0:128], 16, 1)
    own_row[0] = row
    k_p[xc * 8 + z] = row
    k_q[xc * 8 + y] = row

    pltpu.make_async_copy(operators_hbm, operators, op_sem).wait()
    pl.semaphore_wait(barrier, 7 + 14 + 14)

    for step in FAR:
        push(own_row.at[0], k_p.at[xc * 8 + z], send1, k1_sem.at[0], at(x, y, c, around(z, step)))
        push(own_row.at[0], k_q.at[xc * 8 + y], send1, k1_sem.at[1], at(x, around(y, step), c, z))

    def pieces(chunk, dst, sem, device, local):
        for part in range(2):
            col = pl.multiple_of(part * HALF + chunk * CHUNK, 128)
            src = operators.at[0, :, pl.ds(col, CHUNK)]
            if local:
                keep(src, dst.at[part], sem)
            else:
                push(src, dst.at[part], send2, sem, device)

    def offer(step, pc):
        ring = around(z, step)
        live, chunk = held_p(pc, ring)

        @pl.when(live)
        def _():
            pieces(chunk, in_p.at[c * 8 + z], in_sem.at[0], at(x, y, pc, ring), False)

        ring2 = around(y, step)
        live2, chunk2 = held_q(pc, ring2)

        @pl.when(live2)
        def _():
            pieces(chunk2, in_q.at[c * 8 + y], in_sem.at[1], at(x, ring2, pc, z), False)

    for step in FAR:
        offer(step, c)
        offer(step, 1 - c)
    offer(0, 1 - c)

    @pl.when(live_p)
    def _():
        pieces(chunk_p, in_p.at[c * 8 + z], in_sem.at[0], None, True)

    @pl.when(live_q)
    def _():
        pieces(chunk_q, in_q.at[c * 8 + y], in_sem.at[1], None, True)

    settle(k_p.at[pl.ds(0, 7)], k1_sem.at[0])
    settle(k_q.at[pl.ds(0, 7)], k1_sem.at[1])

    for px, pc, _ in columns[:-1]:
        push(k_p.at[pl.ds(xc * 8, 8)], k_p.at[pl.ds(xc * 8, 8)], send1, k2_sem.at[0], at(px, y, pc, z))
        push(k_q.at[pl.ds(xc * 8, 8)], k_q.at[pl.ds(xc * 8, 8)], send1, k2_sem.at[1], at(px, y, pc, z))

    def collect(incoming, gathered, slot, sem, gather_sem, along_y):
        settle(incoming, sem)
        for s in range(16):
            for part in range(2):
                stage[2 * s:2 * s + 2, part * CHUNK:(part + 1) * CHUNK] = incoming[s, part].astype(F32)
        gathered[slot] = stage[...].astype(BF)

        for step in FAR:
            device = at(x, around(y, step), c, z) if along_y else at(x, y, c, around(z, step))
            push(gathered.at[slot], gathered.at[slot], send3, gather_sem, device)

    @pl.when(live_p)
    def _():
        collect(in_p, all_p, y, in_sem.at[0], all_sem.at[0], True)

    @pl.when(live_q)
    def _():
        collect(in_q, all_q, z, in_sem.at[1], all_sem.at[1], False)

    lane = iota((W, 128), 1)

    pltpu.make_async_copy(rvec_hbm, rvec, small_sem.at[0]).wait()
    pltpu.make_async_copy(degen_hbm, degen, small_sem.at[1]).wait()
    settle(k_p.at[pl.ds(0, 56)], k2_sem.at[0])
    settle(k_q.at[pl.ds(0, 56)], k2_sem.at[1])
    lattice_rows = iota((128, NR), 0)
    rv = rvec[...].astype(F32)
    lattice = jnp.where(
        lattice_rows < 8, rv[0:1],
        jnp.where(lattice_rows < 16, rv[1:2], jnp.where(lattice_rows < 24, rv[2:3], 0.0)),
    )
    weight = degen[...].astype(F32)

    @pl.when(live_p)
    def _():
        fold_table(k_p, lattice.astype(BF), 1.0 / weight, tab_p)

    @pl.when(live_q)
    def _():
        col = iota((NR, NR), 1)
        source = (
            lax.rem(lax.div(col, 2), 8) * 32 + lax.rem(lax.div(col, 16), 2) * 16
            + lax.div(col, 32) * 2 + lax.rem(col, 2)
        )
        swap = (iota((NR, NR), 0) == source).astype(F32).astype(BF)
        moved = dot(lattice.astype(BF), swap).astype(BF)
        weights = dot(jnp.broadcast_to(weight, (8, NR)).astype(BF), swap)[0:1]
        fold_table(k_q, moved, 1.0 / weights, tab_q)

    def deliver(chunk, out, along_z, half):
        dst = full.at[half, x, chunk]

        def one(step, some):
            ring = around(z if along_z else y, step)
            for px, pc, pxc in some:
                device = at(px, y, pc, ring) if along_z else at(px, ring, pc, z)
                push(out.at[half, pxc * 8 + ring], dst, send3, full_sem.at[half], device)

        def far(i):
            half = lax.div(i + 1, 2)
            one(jnp.where(lax.rem(i, 2) == 0, 4 + half, 4 - half), columns)

        each(7, far)
        one(0, columns[:-1])
        keep(out.at[half, xc * 8 + (z if along_z else y)], dst, full_sem.at[half])

    @pl.when(live_p)
    def _():
        settle(all_p.at[pl.ds(0, 7)], all_sem.at[0])
        transform(tab_p, all_p, out_p, 0)
        deliver(chunk_p, out_p, True, 0)

    @pl.when(live_q)
    def _():
        settle(all_q.at[pl.ds(0, 7)], all_sem.at[1])
        transform(tab_q, all_q, out_q, 0)
        deliver(chunk_q, out_q, False, 0)

    @pl.when(live_p)
    def _():
        transform(tab_p, all_p, out_p, 1)
        deliver(chunk_p, out_p, True, 1)

    @pl.when(live_q)
    def _():
        transform(tab_q, all_q, out_q, 1)
        deliver(chunk_q, out_q, False, 1)

    pltpu.make_async_copy(vectors, vec, vec_sem).wait()
    for part in range(2):
        def put(i, val, part=part):
            mats[part, i * KPT:(i + 1) * KPT, :] = val

        matrix_rows(lambda t, part=part: vec[:, part * HALF + t * 128: part * HALF + (t + 1) * 128].astype(F32), put)

    def eigen(k):
        vr = mats[0, pl.ds(k, W, stride=KPT), :]
        vi = mats[1, pl.ds(k, W, stride=KPT), :]
        gap = jnp.zeros((48, 256), BF)
        right[k, 0:W, :] = jnp.concatenate([vr, vi], axis=1).astype(BF)
        right[k, W:128, :] = gap
        right[k, 128:128 + W, :] = jnp.concatenate([-vi, vr], axis=1).astype(BF)
        right[k, 128 + W:, :] = gap
        fill = jnp.zeros((48, 128), F32)
        tr = jnp.transpose(jnp.concatenate([vr, fill], axis=0))[:W]
        ti = jnp.transpose(jnp.concatenate([vi, fill], axis=0))[:W]
        left[k] = paired(tr, ti).astype(BF)

    def paired(re, im):
        moved = pltpu.roll(im, W, 1)
        return jnp.concatenate([jnp.where(lane < W, re, moved), moved[:, :2 * W - 128]], axis=1)

    each(KPT, eigen)

    sub = iota((W, 128), 0)

    def rotate(half):
        settle(full.at[half], full_sem.at[half])

        def rebuild(o):
            def put(i, val):
                mats[o, i * KPT:(i + 1) * KPT, :] = val

            matrix_rows(lambda t: full[half, o, t // 2, :, (t % 2) * 128:(t % 2 + 1) * 128].astype(F32), put)

        each(4, rebuild)
        group = range(4)
        prods = []
        for k in group:
            ops = [
                jnp.concatenate(
                    [mats[o, pl.ds(k, W, stride=KPT), :], mats[o, pl.ds(4 + k, W, stride=KPT), :]], axis=1
                ).astype(BF)
                for o in range(4)
            ]
            prods.append(dot(jnp.concatenate(ops, axis=0), right[half * 4 + k]).astype(BF))
        rots = [[] for _ in group]
        for o in range(4):
            for k in group:
                re = prods[k][o * W:(o + 1) * W, :128]
                im = prods[k][o * W:(o + 1) * W, 128:]
                stacked = jnp.concatenate(
                    [jnp.concatenate([re, im], axis=1), jnp.concatenate([im, -re], axis=1)], axis=0
                )
                rots[k].append(dot(left[half * 4 + k], stacked).astype(BF))
        hams, weights = [], []
        for k in group:
            ham_re, ham_im = rots[k][0][:, :128].astype(F32), rots[k][0][:, 128:].astype(F32)
            diag = jnp.where(sub == lane, ham_re, 0.0)
            down = 1.0 / (1.0 + jnp.exp(jnp.sum(diag, axis=1, keepdims=True) * (1.0 / SMEARING)))
            along = 1.0 / (1.0 + jnp.exp(jnp.sum(diag, axis=0, keepdims=True) * (1.0 / SMEARING)))
            weights.append((1.0 - down) * along)
            hams.append(paired(ham_re, ham_im).astype(BF))
        products = [[] for _ in group]
        turned = [[] for _ in group]
        fill = jnp.zeros((48, 128), F32)
        for b in range(3):
            for k in group:
                re, im = rots[k][b + 1][:, :128], rots[k][b + 1][:, 128:]
                stacked = jnp.concatenate(
                    [jnp.concatenate([re, im], axis=1), jnp.concatenate([-im, re], axis=1)], axis=0
                )
                products[k].append(dot(hams[k], stacked))
                turned[k].append((
                    jnp.transpose(jnp.concatenate([re.astype(F32), fill], axis=0))[:W],
                    jnp.transpose(jnp.concatenate([im.astype(F32), fill], axis=0))[:W],
                ))
        spot8 = iota((KPT, 128), 0)
        for comp, (a, b) in enumerate(((1, 2), (2, 0), (0, 1))):
            found = jnp.zeros((KPT, 128), F32)
            for k in group:
                terms = (
                    turned[k][a][0] * products[k][b][:, 128:] + turned[k][a][1] * products[k][b][:, :128]
                    - turned[k][b][0] * products[k][a][:, 128:] - turned[k][b][1] * products[k][a][:, :128]
                ) * weights[k]
                found = jnp.where(spot8 == half * 4 + k, jnp.sum(terms, axis=0, keepdims=True) * (1.0 / W), found)
            stage[comp * KPT:(comp + 1) * KPT, 0:128] = stage[comp * KPT:(comp + 1) * KPT, 0:128] + found

    stage[...] = jnp.zeros_like(stage)
    each(2, rotate)
    spot = iota((1, 128), 1)
    part = jnp.zeros((1, 128), F32)
    for comp in range(3):
        sumk = jnp.sum(stage[comp * KPT:(comp + 1) * KPT, 0:128], axis=0, keepdims=True)
        part = part + jnp.where(spot == comp, jnp.sum(sumk, axis=1, keepdims=True), 0.0)

    sums[xc * 8 + z] = part

    def tell(step, some):
        ring = around(z, step)
        for px, pc, _ in some:
            push(sums.at[xc * 8 + z], sums.at[xc * 8 + z], sum_send, sum_sem.at[0], at(px, y, pc, ring))

    def tell_far(i):
        half = lax.div(i + 1, 2)
        tell(jnp.where(lax.rem(i, 2) == 0, 4 + half, 4 - half), columns)

    each(7, tell_far)
    tell(0, columns[:-1])
    eye = iota((KPT, 128), 0) == iota((KPT, 128), 1)
    for comp in range(3):
        column = jnp.sum(stage[comp * KPT:(comp + 1) * KPT, 0:128], axis=1, keepdims=True)
        density[comp:comp + 1] = jnp.sum(jnp.where(eye, column, 0.0), axis=0, keepdims=True)[:, 0:KPT]
    settle(sums.at[pl.ds(0, 63)], sum_sem.at[0])
    sums2[y] = jnp.sum(sums[:, 0, :], axis=0, keepdims=True)
    for step in FAR:
        push(sums2.at[y], sums2.at[y], sum_send, sum_sem.at[1], at(x, around(y, step), c, z))
    settle(sums2.at[pl.ds(0, 7)], sum_sem.at[1])
    part = jnp.sum(sums2[:, 0, :], axis=0, keepdims=True)
    magnet[...] = part[:, 0:3] * (1.0 / KPOINTS)

    settle(sums.at[pl.ds(0, 63)], sum_send)
    settle(sums2.at[pl.ds(0, 7)], sum_send)
    settle(k_p.at[pl.ds(0, 14)], send1)
    settle(k_p.at[pl.ds(0, 56)], send1)
    settle(k_p.at[pl.ds(0, 56)], send1)

    settle(in_p.at[pl.ds(0, 12)], send2)

    @pl.when(jnp.logical_not(live_p))
    def _():
        settle(in_p.at[pl.ds(0, 1)], send2)

    settle(in_q.at[pl.ds(0, 11)], send2)

    @pl.when(jnp.logical_not(live_q))
    def _():
        settle(in_q.at[pl.ds(0, 1)], send2)

    @pl.when(live_p)
    def _():
        settle(all_p.at[pl.ds(0, 7)], send3)
        for half in range(2):
            settle(out_p.at[half, pl.ds(0, 63)], send3)

    @pl.when(live_q)
    def _():
        settle(all_q.at[pl.ds(0, 7)], send3)
        for half in range(2):
            settle(out_q.at[half, pl.ds(0, 63)], send3)


def per_device(kgrid, rvec, degen, operators, vectors):
    vmem = pl.BlockSpec(memory_space=pltpu.VMEM)
    anywhere = pl.BlockSpec(memory_space=pl.ANY)
    dma = pltpu.SemaphoreType.DMA
    density, magnet = pl.pallas_call(
        body,
        out_shape=(pltpu.VMEM((3, KPT), F32), pltpu.VMEM((1, 3), F32)),
        in_specs=[anywhere] * 5,
        out_specs=(vmem, vmem),
        scratch_shapes=[
            pltpu.VMEM((3, KPT), jnp.int32),
            pltpu.VMEM((3, NR), jnp.int32),
            pltpu.VMEM((1, NR), jnp.int32),
            pltpu.VMEM((1, 2, 2 * HALF), BF),
            pltpu.VMEM((KPT, 2 * HALF), BF),
            pltpu.VMEM((1, 1, 128), F32),
            pltpu.VMEM((64, 1, 128), F32),
            pltpu.VMEM((64, 1, 128), F32),
            pltpu.VMEM((16, 2, 2, CHUNK), BF),
            pltpu.VMEM((16, 2, 2, CHUNK), BF),
            pltpu.VMEM((32, 2 * CHUNK), F32),
            pltpu.VMEM((RING, 32, 2 * CHUNK), BF),
            pltpu.VMEM((RING, 32, 2 * CHUNK), BF),
            pltpu.VMEM((1024, 2 * NR), BF),
            pltpu.VMEM((1024, 2 * NR), BF),
            pltpu.VMEM((2, 64, KPT, CHUNK), BF),
            pltpu.VMEM((2, 64, KPT, CHUNK), BF),
            pltpu.VMEM((2, 4, CHUNKS, KPT, CHUNK), BF),
            pltpu.VMEM((4, W * KPT, 128), F32),
            pltpu.VMEM((KPT, 256, 256), BF),
            pltpu.VMEM((KPT, W, 2 * W), BF),
            pltpu.VMEM((64, 1, 128), F32),
            pltpu.VMEM((8, 1, 128), F32),
            dma, dma, dma, dma((2,)), dma((2,)), dma((2,)), dma((2,)), dma((2,)), dma, dma, dma((2,)), dma, dma((2,)), dma,
        ],
        compiler_params=pltpu.CompilerParams(
            collective_id=0, has_side_effects=True, vmem_limit_bytes=56 * 1024 * 1024
        ),
        name="orbital",
    )(kgrid, rvec, degen.reshape(1, NR), operators, vectors)
    return density, magnet.reshape(3)


def solution(mesh):
    return jax.shard_map(
        per_device,
        mesh=mesh,
        in_specs=(P(None, ("ka", "op", "row")), P(), P(), P("op", ("ka", "row"), None), P(("ka", "op", "row"), None)),
        out_specs=(P(None, ("ka", "op", "row")), P()),
        check_vma=False,
    )
```

```python
import functools
import math

import jax
import jax.numpy as jnp
from jax import lax
from jax.experimental import pallas as pl
from jax.experimental.pallas import tpu as pltpu
from jax.sharding import PartitionSpec as P

W = 80
GRID = 64
SMEARING = 0.5
NX, NY, NZ, NC = 4, 8, 8, 2
XC = NX * NC
RING = 8
KPT = 8
NR = 256
HALF = W * W
CHUNK = 256
CHUNKS = HALF // CHUNK
FIRST_Q = 13
KPOINTS = 4096
MESH = pl.DeviceIdType.MESH
BF = jnp.bfloat16
F32 = jnp.float32


def place():
    ka = lax.axis_index("ka")
    return lax.axis_index("op"), lax.div(ka, 2), lax.rem(ka, 2), lax.axis_index("row")


def at(x, y, c, z):
    return (2 * y + c, x, z)


def held_p(c, z):
    live = (c == 0) | (lax.rem(z, 2) == 0) | (z == 7)
    return live, jnp.where(c == 0, z, 8 + lax.div(z + 1, 2))


def held_q(c, y):
    live = (c == 1) | (lax.rem(y, 2) == 0)
    return live, FIRST_Q + jnp.where(c == 1, y, 8 + lax.div(y, 2))


FAR = (4, 3, 5, 2, 6, 1, 7)


def settle(ref, sem):
    pltpu.make_async_copy(ref, ref, sem).wait()


def push(src, dst, send_sem, recv_sem, device):
    pltpu.make_async_remote_copy(
        src_ref=src, dst_ref=dst, send_sem=send_sem, recv_sem=recv_sem,
        device_id=device, device_id_type=MESH,
    ).start()


def keep(src, dst, sem):
    pltpu.make_async_copy(src, dst, sem).start()


def each(count, body):
    def step(i, carry):
        body(i)
        return carry

    lax.fori_loop(0, count, step, 0)


def around(place, step):
    return lax.rem(place + step, RING)


def partners(x, c):
    order = ((2, 0), (2, 1), (1, 0), (3, 0), (1, 1), (3, 1), (0, 1), (0, 0))
    found = []
    for dx, dc in order:
        px, pc = lax.rem(x + dx, NX), (1 - c if dc else c)
        found.append((px, pc, 2 * px + pc))
    return found


def iota(shape, dim):
    return lax.broadcasted_iota(jnp.int32, shape, dim)


def dot(a, b):
    return jnp.dot(a, b, preferred_element_type=F32)


def matrix_rows(tile, put):
    lane = iota((KPT, 128), 1)
    for i in range(W):
        first, off = divmod(i * W, 128)
        row = tile(first)
        if off:
            row = pltpu.roll(row, 128 - off, 1)
            if off + W > 128:
                nxt = pltpu.roll(tile(first + 1), 128 - off, 1)
                row = jnp.where(lane < 128 - off, row, nxt)
        put(i, jnp.where(lane < W, row, 0.0))


def fold_table(rows_ref, lattice, inverse, table):
    points = rows_ref[:, 0, :]
    spread = (lax.div(iota((256, 64), 0), 4) == iota((256, 64), 1)).astype(F32).astype(BF)
    wide = dot(spread, points.astype(BF))
    first = lax.rem(iota((128, NR), 0), 8) < 4
    for block in range(4):
        half, rows = block // 2, slice((block % 2) * 128, (block % 2 + 1) * 128)
        own = half * 4 + lax.rem(iota((128, 128), 0), 4) == lax.rem(iota((128, 128), 1), 8)
        winding = dot(jnp.where(own, wide[rows], 0.0).astype(BF), lattice)
        winding = winding - GRID * jnp.floor(winding * (1.0 / GRID))
        upper = winding >= GRID // 2
        turn = jnp.where(upper, winding - (GRID // 2), winding) - (GRID // 4)
        sign = jnp.where(upper, inverse, -inverse)
        angle = turn * (2.0 * math.pi / GRID)
        sq = angle * angle
        odd = -1.0 / 39916800.0
        for term in (1.0 / 362880.0, -1.0 / 5040.0, 1.0 / 120.0, -1.0 / 6.0, 1.0):
            odd = odd * sq + term
        even = 1.0 / 479001600.0
        for term in (-1.0 / 3628800.0, 1.0 / 40320.0, -1.0 / 720.0, 1.0 / 24.0, -0.5, 1.0):
            even = even * sq + term
        cosine = odd * angle * sign
        minus = even * sign
        pairs = []
        for upper_part, lower_part in ((cosine, -minus), (minus, cosine)):
            swapped_low = swap4(lower_part)
            swapped_up = swap4(upper_part)
            even_slot = jnp.where(first, upper_part, swapped_low).reshape(16, 1, 8, NR)
            odd_slot = jnp.where(first, swapped_up, lower_part).reshape(16, 1, 8, NR)
            pairs.append(jnp.concatenate([even_slot, odd_slot], axis=1).reshape(256, NR))
        table[block * 256:(block + 1) * 256, :NR] = pairs[0].astype(BF)
        table[block * 256:(block + 1) * 256, NR:] = pairs[1].astype(BF)


def swap4(val):
    return pltpu.roll(val.reshape(16, 8, NR), 4, 1).reshape(128, NR)


def transform(table, gathered, out, side, half):
    for part in range(2):
        rows = slice(half * 512 + part * 256, half * 512 + (part + 1) * 256)
        block = gathered[side].reshape(NR, 2 * 128)
        total = dot(table[rows, :NR], block[:, :128]) + dot(table[rows, NR:], block[:, 128:])
        out[half, side, part * 32:(part + 1) * 32] = total.reshape(32, KPT, 128).astype(BF)


def body(
    kgrid_hbm, rvec_hbm, degen_hbm, operators_hbm, vectors, result,
    kgrid, rvec, degen, operators, vec, own_row, k_p, k_q, in_p, in_q, stage, all_p, all_q, tab_p, tab_q,
    out_p, out_q, full, mats, right, left, sums, sums2,
    send1, send2, send3, k1_sem, k2_sem, in_sem, p_sem, q_sem, full_sem, vec_sem, sum_send, sum_sem, kg_sem, small_sem, op_sem,
):
    x, y, c, z = place()
    xc = 2 * x + c
    live_p, chunk_p = held_p(c, z)
    live_q, chunk_q = held_q(c, y)
    barrier = pltpu.get_barrier_semaphore()
    keep(kgrid_hbm, kgrid, kg_sem)
    keep(rvec_hbm, rvec, small_sem.at[0])
    keep(degen_hbm, degen, small_sem.at[1])
    keep(operators_hbm, operators, op_sem)
    keep(vectors, vec, vec_sem)
    columns = partners(x, c)

    for px, pc, _ in columns[:-1]:
        pl.semaphore_signal(barrier, inc=1, device_id=at(px, y, pc, z), device_id_type=MESH)
    for step in FAR:
        for pc in (c, 1 - c):
            pl.semaphore_signal(barrier, inc=1, device_id=at(x, y, pc, around(z, step)), device_id_type=MESH)
            pl.semaphore_signal(barrier, inc=1, device_id=at(x, around(y, step), pc, z), device_id_type=MESH)
    pltpu.make_async_copy(kgrid_hbm, kgrid, kg_sem).wait()

    stage[...] = jnp.zeros_like(stage)
    stage[0:3, 0:KPT] = kgrid[...].astype(F32)
    row = stage[0:1, 0:128]
    row = row + pltpu.roll(stage[1:2, 0:128], 8, 1) + pltpu.roll(stage[2:3, 0:128], 16, 1)
    own_row[0] = row
    k_p[xc * 8 + z] = row
    k_q[xc * 8 + y] = row

    pltpu.make_async_copy(operators_hbm, operators, op_sem).wait()
    pl.semaphore_wait(barrier, 7 + 14 + 14)

    def pieces(chunk, dst, sem, device, local):
        for part in range(2):
            col = pl.multiple_of(part * HALF + chunk * CHUNK, 128)
            src = operators.at[0, :, pl.ds(col, CHUNK)]
            if local:
                keep(src, dst.at[part], sem)
            else:
                push(src, dst.at[part], send2, sem, device)

    def offer(step, pc):
        ring = around(z, step)
        live, chunk = held_p(pc, ring)

        @pl.when(live)
        def _():
            pieces(chunk, in_p.at[c * 8 + z], in_sem.at[0], at(x, y, pc, ring), False)

        ring2 = around(y, step)
        live2, chunk2 = held_q(pc, ring2)

        @pl.when(live2)
        def _():
            pieces(chunk2, in_q.at[c * 8 + y], in_sem.at[1], at(x, ring2, pc, z), False)

    for step in FAR:
        offer(step, c)
        offer(step, 1 - c)
    offer(0, 1 - c)

    @pl.when(live_p)
    def _():
        pieces(chunk_p, in_p.at[c * 8 + z], in_sem.at[0], None, True)

    @pl.when(live_q)
    def _():
        pieces(chunk_q, in_q.at[c * 8 + y], in_sem.at[1], None, True)

    for step in FAR:
        push(own_row.at[0], k_p.at[xc * 8 + z], send1, k1_sem.at[0], at(x, y, c, around(z, step)))
        push(own_row.at[0], k_q.at[xc * 8 + y], send1, k1_sem.at[1], at(x, around(y, step), c, z))

    settle(k_p.at[pl.ds(0, 7)], k1_sem.at[0])
    settle(k_q.at[pl.ds(0, 7)], k1_sem.at[1])

    for px, pc, _ in columns[:-1]:
        push(k_p.at[pl.ds(xc * 8, 8)], k_p.at[pl.ds(xc * 8, 8)], send1, k2_sem.at[0], at(px, y, pc, z))
        push(k_q.at[pl.ds(xc * 8, 8)], k_q.at[pl.ds(xc * 8, 8)], send1, k2_sem.at[1], at(px, y, pc, z))

    def collect(incoming, gathered, slot, sem, gather_sem, along_y):
        settle(incoming, sem)
        for s in range(16):
            for part in range(2):
                stage[2 * s:2 * s + 2, part * CHUNK:(part + 1) * CHUNK] = incoming[s, part].astype(F32)
        for side in range(2):
            own = slice(side * 128, side * 128 + 128), slice(CHUNK + side * 128, CHUNK + side * 128 + 128)
            gathered[side, slot] = jnp.concatenate([stage[:, own[0]], stage[:, own[1]]], axis=1).astype(BF)

        for side in range(2):
            for step in FAR:
                device = at(x, around(y, step), c, z) if along_y else at(x, y, c, around(z, step))
                push(gathered.at[side, slot], gathered.at[side, slot], send3, gather_sem.at[side], device)

    @pl.when(live_p)
    def _():
        collect(in_p, all_p, y, in_sem.at[0], p_sem, True)

    @pl.when(live_q)
    def _():
        collect(in_q, all_q, z, in_sem.at[1], q_sem, False)

    lane = iota((W, 128), 1)

    pltpu.make_async_copy(rvec_hbm, rvec, small_sem.at[0]).wait()
    pltpu.make_async_copy(degen_hbm, degen, small_sem.at[1]).wait()
    settle(k_p.at[pl.ds(0, 56)], k2_sem.at[0])
    settle(k_q.at[pl.ds(0, 56)], k2_sem.at[1])
    lattice_rows = iota((128, NR), 0)
    rv = rvec[...].astype(F32)
    lattice = jnp.where(
        lattice_rows < 8, rv[0:1],
        jnp.where(lattice_rows < 16, rv[1:2], jnp.where(lattice_rows < 24, rv[2:3], 0.0)),
    )
    weight = degen[...].astype(F32)

    @pl.when(live_p)
    def _():
        fold_table(k_p, lattice.astype(BF), 1.0 / weight, tab_p)

    @pl.when(live_q)
    def _():
        col = iota((NR, NR), 1)
        source = (
            lax.rem(lax.div(col, 2), 8) * 32 + lax.rem(lax.div(col, 16), 2) * 16
            + lax.div(col, 32) * 2 + lax.rem(col, 2)
        )
        swap = (iota((NR, NR), 0) == source).astype(F32).astype(BF)
        moved = dot(lattice.astype(BF), swap).astype(BF)
        weights = dot(jnp.broadcast_to(weight, (8, NR)).astype(BF), swap)[0:1]
        fold_table(k_q, moved, 1.0 / weights, tab_q)

    def deliver(chunk, out, along_z, side, half):
        dst = full.at[half, x, chunk, side]
        sem = full_sem.at[half]

        def one(step, some):
            ring = around(z if along_z else y, step)
            for px, pc, pxc in some:
                device = at(px, y, pc, ring) if along_z else at(px, ring, pc, z)
                push(out.at[half, side, pxc * 8 + ring], dst, send3, sem, device)

        for step in FAR:
            one(step, columns)
        one(0, columns[:-1])
        keep(out.at[half, side, xc * 8 + (z if along_z else y)], dst, sem)

    def serve_p(side, half):
        @pl.when(live_p)
        def _():
            if half == 0:
                settle(all_p.at[side, pl.ds(0, 7)], p_sem.at[side])
            transform(tab_p, all_p, out_p, side, half)
            deliver(chunk_p, out_p, True, side, half)

    def serve_q(side, half):
        @pl.when(live_q)
        def _():
            if half == 0:
                settle(all_q.at[side, pl.ds(0, 7)], q_sem.at[side])
            transform(tab_q, all_q, out_q, side, half)
            deliver(chunk_q, out_q, False, side, half)

    for side in range(2):
        for half in range(2):
            serve_p(side, half)
            serve_q(side, half)

    pltpu.make_async_copy(vectors, vec, vec_sem).wait()
    for part in range(2):
        def put(i, val, part=part):
            mats[part, i * KPT:(i + 1) * KPT, :] = val

        matrix_rows(lambda t, part=part: vec[:, part * HALF + t * 128: part * HALF + (t + 1) * 128].astype(F32), put)

    def eigen(k):
        vr = mats[0, pl.ds(k, W, stride=KPT), :]
        vi = mats[1, pl.ds(k, W, stride=KPT), :]
        gap = jnp.zeros((48, 256), BF)
        right[k, 0:W, :] = jnp.concatenate([vr, vi], axis=1).astype(BF)
        right[k, W:128, :] = gap
        right[k, 128:128 + W, :] = jnp.concatenate([-vi, vr], axis=1).astype(BF)
        right[k, 128 + W:, :] = gap
        fill = jnp.zeros((48, 128), F32)
        tr = jnp.transpose(jnp.concatenate([vr, fill], axis=0))[:W]
        ti = jnp.transpose(jnp.concatenate([vi, fill], axis=0))[:W]
        left[k] = paired(tr, ti).astype(BF)

    def paired(re, im):
        moved = pltpu.roll(im, W, 1)
        return jnp.concatenate([jnp.where(lane < W, re, moved), moved[:, :2 * W - 128]], axis=1)

    each(KPT, eigen)

    sub = iota((W, 128), 0)

    def rotate(half):
        settle(full.at[half], full_sem.at[half])

        def rebuild(o):
            def put(i, val):
                mats[o, i * KPT:(i + 1) * KPT, :] = val

            matrix_rows(lambda t: full[half, o, t // 2, t % 2].astype(F32), put)

        each(4, rebuild)
        group = range(4)
        prods = []
        for k in group:
            ops = [
                jnp.concatenate(
                    [mats[o, pl.ds(k, W, stride=KPT), :], mats[o, pl.ds(4 + k, W, stride=KPT), :]], axis=1
                ).astype(BF)
                for o in range(4)
            ]
            prods.append(dot(jnp.concatenate(ops, axis=0), right[half * 4 + k]).astype(BF))
        rots = [[] for _ in group]
        for o in range(4):
            for k in group:
                re = prods[k][o * W:(o + 1) * W, :128]
                im = prods[k][o * W:(o + 1) * W, 128:]
                stacked = jnp.concatenate(
                    [jnp.concatenate([re, im], axis=1), jnp.concatenate([im, -re], axis=1)], axis=0
                )
                rots[k].append(dot(left[half * 4 + k], stacked).astype(BF))
        hams, weights = [], []
        for k in group:
            ham_re, ham_im = rots[k][0][:, :128].astype(F32), rots[k][0][:, 128:].astype(F32)
            diag = jnp.where(sub == lane, ham_re, 0.0)
            down = 1.0 / (1.0 + jnp.exp(jnp.sum(diag, axis=1, keepdims=True) * (1.0 / SMEARING)))
            along = 1.0 / (1.0 + jnp.exp(jnp.sum(diag, axis=0, keepdims=True) * (1.0 / SMEARING)))
            weights.append((1.0 - down) * along)
            hams.append(paired(ham_re, ham_im).astype(BF))
        products = [[] for _ in group]
        turned = [[] for _ in group]
        fill = jnp.zeros((48, 128), F32)
        for b in range(3):
            for k in group:
                re, im = rots[k][b + 1][:, :128], rots[k][b + 1][:, 128:]
                stacked = jnp.concatenate(
                    [jnp.concatenate([re, im], axis=1), jnp.concatenate([-im, re], axis=1)], axis=0
                )
                products[k].append(dot(hams[k], stacked))
                turned[k].append((
                    jnp.transpose(jnp.concatenate([re.astype(F32), fill], axis=0))[:W],
                    jnp.transpose(jnp.concatenate([im.astype(F32), fill], axis=0))[:W],
                ))
        spot8 = iota((KPT, 128), 0)
        for comp, (a, b) in enumerate(((1, 2), (2, 0), (0, 1))):
            found = jnp.zeros((KPT, 128), F32)
            for k in group:
                terms = (
                    turned[k][a][0] * products[k][b][:, 128:] + turned[k][a][1] * products[k][b][:, :128]
                    - turned[k][b][0] * products[k][a][:, 128:] - turned[k][b][1] * products[k][a][:, :128]
                ) * weights[k]
                found = jnp.where(spot8 == half * 4 + k, jnp.sum(terms, axis=0, keepdims=True) * (1.0 / W), found)
            stage[comp * KPT:(comp + 1) * KPT, 0:128] = stage[comp * KPT:(comp + 1) * KPT, 0:128] + found

    stage[...] = jnp.zeros_like(stage)
    each(2, rotate)
    spot = iota((1, 128), 1)
    part = jnp.zeros((1, 128), F32)
    for comp in range(3):
        sumk = jnp.sum(stage[comp * KPT:(comp + 1) * KPT, 0:128], axis=0, keepdims=True)
        part = part + jnp.where(spot == comp, jnp.sum(sumk, axis=1, keepdims=True), 0.0)

    sums[xc * 8 + z] = part

    def tell(step, some):
        ring = around(z, step)
        for px, pc, _ in some:
            push(sums.at[xc * 8 + z], sums.at[xc * 8 + z], sum_send, sum_sem.at[0], at(px, y, pc, ring))

    def tell_far(i):
        half = lax.div(i + 1, 2)
        tell(jnp.where(lax.rem(i, 2) == 0, 4 + half, 4 - half), columns)

    each(7, tell_far)
    tell(0, columns[:-1])
    eye = iota((KPT, 128), 0) == iota((KPT, 128), 1)
    for comp in range(3):
        column = jnp.sum(stage[comp * KPT:(comp + 1) * KPT, 0:128], axis=1, keepdims=True)
        result[comp:comp + 1] = jnp.sum(jnp.where(eye, column, 0.0), axis=0, keepdims=True)
    settle(sums.at[pl.ds(0, 63)], sum_sem.at[0])
    sums2[y] = jnp.sum(sums[:, 0, :], axis=0, keepdims=True)
    for step in FAR:
        push(sums2.at[y], sums2.at[y], sum_send, sum_sem.at[1], at(x, around(y, step), c, z))
    settle(sums2.at[pl.ds(0, 7)], sum_sem.at[1])
    part = jnp.sum(sums2[:, 0, :], axis=0, keepdims=True)
    result[3:4] = part * (1.0 / KPOINTS)

    settle(sums.at[pl.ds(0, 63)], sum_send)
    settle(sums2.at[pl.ds(0, 7)], sum_send)
    settle(k_p.at[pl.ds(0, 14)], send1)
    settle(k_p.at[pl.ds(0, 56)], send1)
    settle(k_p.at[pl.ds(0, 56)], send1)

    settle(in_p.at[pl.ds(0, 12)], send2)

    @pl.when(jnp.logical_not(live_p))
    def _():
        settle(in_p.at[pl.ds(0, 1)], send2)

    settle(in_q.at[pl.ds(0, 11)], send2)

    @pl.when(jnp.logical_not(live_q))
    def _():
        settle(in_q.at[pl.ds(0, 1)], send2)

    @pl.when(live_p)
    def _():
        for side in range(2):
            settle(all_p.at[side, pl.ds(0, 7)], send3)
        for half in range(2):
            for side in range(2):
                settle(out_p.at[half, side, pl.ds(0, 63)], send3)

    @pl.when(live_q)
    def _():
        for side in range(2):
            settle(all_q.at[side, pl.ds(0, 7)], send3)
        for half in range(2):
            for side in range(2):
                settle(out_q.at[half, side, pl.ds(0, 63)], send3)


def per_device(kgrid, rvec, degen, operators, vectors):
    vmem = pl.BlockSpec(memory_space=pltpu.VMEM)
    anywhere = pl.BlockSpec(memory_space=pl.ANY)
    dma = pltpu.SemaphoreType.DMA
    result = pl.pallas_call(
        body,
        out_shape=pltpu.VMEM((8, 128), F32),
        in_specs=[anywhere] * 5,
        out_specs=vmem,
        scratch_shapes=[
            pltpu.VMEM((3, KPT), jnp.int32),
            pltpu.VMEM((3, NR), jnp.int32),
            pltpu.VMEM((1, NR), jnp.int32),
            pltpu.VMEM((1, 2, 2 * HALF), BF),
            pltpu.VMEM((KPT, 2 * HALF), BF),
            pltpu.VMEM((1, 1, 128), F32),
            pltpu.VMEM((64, 1, 128), F32),
            pltpu.VMEM((64, 1, 128), F32),
            pltpu.VMEM((16, 2, 2, CHUNK), BF),
            pltpu.VMEM((16, 2, 2, CHUNK), BF),
            pltpu.VMEM((32, 2 * CHUNK), F32),
            pltpu.VMEM((2, RING, 32, CHUNK), BF),
            pltpu.VMEM((2, RING, 32, CHUNK), BF),
            pltpu.VMEM((1024, 2 * NR), BF),
            pltpu.VMEM((1024, 2 * NR), BF),
            pltpu.VMEM((2, 2, 64, KPT, 128), BF),
            pltpu.VMEM((2, 2, 64, KPT, 128), BF),
            pltpu.VMEM((2, 4, CHUNKS, 2, KPT, 128), BF),
            pltpu.VMEM((4, W * KPT, 128), F32),
            pltpu.VMEM((KPT, 256, 256), BF),
            pltpu.VMEM((KPT, W, 2 * W), BF),
            pltpu.VMEM((64, 1, 128), F32),
            pltpu.VMEM((8, 1, 128), F32),
            dma, dma, dma, dma((2,)), dma((2,)), dma((2,)), dma((2,)), dma((2,)), dma((2,)), dma, dma, dma((2,)), dma, dma((2,)), dma,
        ],
        compiler_params=pltpu.CompilerParams(
            collective_id=0, has_side_effects=True, vmem_limit_bytes=56 * 1024 * 1024
        ),
        name="orbital",
    )(kgrid, rvec, degen.reshape(1, NR), operators, vectors)
    return result[0:3, 0:KPT], result[3, 0:3]


def solution(mesh):
    return jax.shard_map(
        per_device,
        mesh=mesh,
        in_specs=(P(None, ("ka", "op", "row")), P(), P(), P("op", ("ka", "row"), None), P(("ka", "op", "row"), None)),
        out_specs=(P(None, ("ka", "op", "row")), P()),
        check_vma=False,
    )
```

```python
import functools
import math

import jax
import jax.numpy as jnp
from jax import lax
from jax.experimental import pallas as pl
from jax.experimental.pallas import tpu as pltpu
from jax.sharding import PartitionSpec as P

W = 80
GRID = 64
SMEARING = 0.5
NX, NY, NZ, NC = 4, 8, 8, 2
XC = NX * NC
RING = 8
KPT = 8
NR = 256
HALF = W * W
CHUNK = 256
CHUNKS = HALF // CHUNK
FIRST_Q = 13
KPOINTS = 4096
MESH = pl.DeviceIdType.MESH
BF = jnp.bfloat16
F32 = jnp.float32


def place():
    ka = lax.axis_index("ka")
    return lax.axis_index("op"), lax.div(ka, 2), lax.rem(ka, 2), lax.axis_index("row")


def at(x, y, c, z):
    return (2 * y + c, x, z)


def held_p(c, z):
    live = (c == 0) | (lax.rem(z, 2) == 0) | (z == 7)
    return live, jnp.where(c == 0, z, 8 + lax.div(z + 1, 2))


def held_q(c, y):
    live = (c == 1) | (lax.rem(y, 2) == 0)
    return live, FIRST_Q + jnp.where(c == 1, y, 8 + lax.div(y, 2))


FAR = (4, 3, 5, 2, 6, 1, 7)


def settle(ref, sem):
    pltpu.make_async_copy(ref, ref, sem).wait()


def push(src, dst, send_sem, recv_sem, device):
    pltpu.make_async_remote_copy(
        src_ref=src, dst_ref=dst, send_sem=send_sem, recv_sem=recv_sem,
        device_id=device, device_id_type=MESH,
    ).start()


def keep(src, dst, sem):
    pltpu.make_async_copy(src, dst, sem).start()


def each(count, body):
    def step(i, carry):
        body(i)
        return carry

    lax.fori_loop(0, count, step, 0)


def around(place, step):
    return lax.rem(place + step, RING)


def partners(x, c):
    order = ((2, 0), (2, 1), (1, 0), (3, 0), (1, 1), (3, 1), (0, 1), (0, 0))
    found = []
    for dx, dc in order:
        px, pc = lax.rem(x + dx, NX), (1 - c if dc else c)
        found.append((px, pc, 2 * px + pc))
    return found


def iota(shape, dim):
    return lax.broadcasted_iota(jnp.int32, shape, dim)


def dot(a, b):
    return jnp.dot(a, b, preferred_element_type=F32)


def matrix_rows(tile, put):
    lane = iota((KPT, 128), 1)
    for i in range(W):
        first, off = divmod(i * W, 128)
        row = tile(first)
        if off:
            row = pltpu.roll(row, 128 - off, 1)
            if off + W > 128:
                nxt = pltpu.roll(tile(first + 1), 128 - off, 1)
                row = jnp.where(lane < 128 - off, row, nxt)
        put(i, jnp.where(lane < W, row, 0.0))


def fold_table(rows_ref, lattice, inverse, table):
    points = rows_ref[:, 0, :]
    spread = (lax.div(iota((256, 64), 0), 4) == iota((256, 64), 1)).astype(F32).astype(BF)
    wide = dot(spread, points.astype(BF))
    first = lax.rem(iota((128, NR), 0), 8) < 4
    for block in range(4):
        half, rows = block // 2, slice((block % 2) * 128, (block % 2 + 1) * 128)
        own = half * 4 + lax.rem(iota((128, 128), 0), 4) == lax.rem(iota((128, 128), 1), 8)
        winding = dot(jnp.where(own, wide[rows], 0.0).astype(BF), lattice)
        winding = winding - GRID * jnp.floor(winding * (1.0 / GRID))
        upper = winding >= GRID // 2
        turn = jnp.where(upper, winding - (GRID // 2), winding) - (GRID // 4)
        sign = jnp.where(upper, inverse, -inverse)
        angle = turn * (2.0 * math.pi / GRID)
        sq = angle * angle
        odd = -1.0 / 39916800.0
        for term in (1.0 / 362880.0, -1.0 / 5040.0, 1.0 / 120.0, -1.0 / 6.0, 1.0):
            odd = odd * sq + term
        even = 1.0 / 479001600.0
        for term in (-1.0 / 3628800.0, 1.0 / 40320.0, -1.0 / 720.0, 1.0 / 24.0, -0.5, 1.0):
            even = even * sq + term
        cosine = odd * angle * sign
        minus = even * sign
        pairs = []
        for upper_part, lower_part in ((cosine, -minus), (minus, cosine)):
            swapped_low = swap4(lower_part)
            swapped_up = swap4(upper_part)
            even_slot = jnp.where(first, upper_part, swapped_low).reshape(16, 1, 8, NR)
            odd_slot = jnp.where(first, swapped_up, lower_part).reshape(16, 1, 8, NR)
            pairs.append(jnp.concatenate([even_slot, odd_slot], axis=1).reshape(256, NR))
        table[block * 256:(block + 1) * 256, :NR] = pairs[0].astype(BF)
        table[block * 256:(block + 1) * 256, NR:] = pairs[1].astype(BF)


def swap4(val):
    return pltpu.roll(val.reshape(16, 8, NR), 4, 1).reshape(128, NR)


def transform(table, gathered, out, side, half):
    for part in range(2):
        rows = slice(half * 512 + part * 256, half * 512 + (part + 1) * 256)
        block = gathered[side].reshape(NR, 2 * 128)
        total = dot(table[rows, :NR], block[:, :128]) + dot(table[rows, NR:], block[:, 128:])
        out[half, side, part * 32:(part + 1) * 32] = total.reshape(32, KPT, 128).astype(BF)


def body(
    kgrid_hbm, rvec_hbm, degen_hbm, operators_hbm, vectors, result,
    kgrid, rvec, degen, operators, vec, own_row, k_p, k_q, in_p, in_q, stage, all_p, all_q, tab_p, tab_q,
    out_p, out_q, full, mats, right, left, sums, sums2,
    send1, send2, send3, k1_sem, k2_sem, in_sem, p_sem, q_sem, full_sem, vec_sem, sum_send, sum_sem, kg_sem, small_sem, op_sem,
):
    x, y, c, z = place()
    xc = 2 * x + c
    live_p, chunk_p = held_p(c, z)
    live_q, chunk_q = held_q(c, y)
    barrier = pltpu.get_barrier_semaphore()
    keep(kgrid_hbm, kgrid, kg_sem)
    keep(rvec_hbm, rvec, small_sem.at[0])
    keep(degen_hbm, degen, small_sem.at[1])
    keep(operators_hbm, operators, op_sem)
    keep(vectors, vec, vec_sem)
    columns = partners(x, c)

    for px, pc, _ in columns[:-1]:
        pl.semaphore_signal(barrier, inc=1, device_id=at(px, y, pc, z), device_id_type=MESH)
    for step in FAR:
        for pc in (c, 1 - c):
            pl.semaphore_signal(barrier, inc=1, device_id=at(x, y, pc, around(z, step)), device_id_type=MESH)
            pl.semaphore_signal(barrier, inc=1, device_id=at(x, around(y, step), pc, z), device_id_type=MESH)
    pltpu.make_async_copy(kgrid_hbm, kgrid, kg_sem).wait()

    stage[...] = jnp.zeros_like(stage)
    stage[0:3, 0:KPT] = kgrid[...].astype(F32)
    row = stage[0:1, 0:128]
    row = row + pltpu.roll(stage[1:2, 0:128], 8, 1) + pltpu.roll(stage[2:3, 0:128], 16, 1)
    own_row[0] = row
    k_p[xc * 8 + z] = row
    k_q[xc * 8 + y] = row

    pltpu.make_async_copy(operators_hbm, operators, op_sem).wait()
    pl.semaphore_wait(barrier, 7 + 14 + 14)

    def pieces(chunk, dst, sem, device, local):
        for part in range(2):
            col = pl.multiple_of(part * HALF + chunk * CHUNK, 128)
            src = operators.at[0, :, pl.ds(col, CHUNK)]
            if local:
                keep(src, dst.at[part], sem)
            else:
                push(src, dst.at[part], send2, sem, device)

    def offer(step, pc):
        ring = around(z, step)
        live, chunk = held_p(pc, ring)

        @pl.when(live)
        def _():
            pieces(chunk, in_p.at[c * 8 + z], in_sem.at[0], at(x, y, pc, ring), False)

        ring2 = around(y, step)
        live2, chunk2 = held_q(pc, ring2)

        @pl.when(live2)
        def _():
            pieces(chunk2, in_q.at[c * 8 + y], in_sem.at[1], at(x, ring2, pc, z), False)

    for step in FAR:
        offer(step, c)
        offer(step, 1 - c)
    offer(0, 1 - c)

    @pl.when(live_p)
    def _():
        pieces(chunk_p, in_p.at[c * 8 + z], in_sem.at[0], None, True)

    @pl.when(live_q)
    def _():
        pieces(chunk_q, in_q.at[c * 8 + y], in_sem.at[1], None, True)

    for step in FAR:
        push(own_row.at[0], k_p.at[xc * 8 + z], send1, k1_sem.at[0], at(x, y, c, around(z, step)))
        push(own_row.at[0], k_q.at[xc * 8 + y], send1, k1_sem.at[1], at(x, around(y, step), c, z))

    settle(k_p.at[pl.ds(0, 7)], k1_sem.at[0])
    settle(k_q.at[pl.ds(0, 7)], k1_sem.at[1])

    for px, pc, _ in columns[:-1]:
        push(k_p.at[pl.ds(xc * 8, 8)], k_p.at[pl.ds(xc * 8, 8)], send1, k2_sem.at[0], at(px, y, pc, z))
        push(k_q.at[pl.ds(xc * 8, 8)], k_q.at[pl.ds(xc * 8, 8)], send1, k2_sem.at[1], at(px, y, pc, z))

    def collect(incoming, gathered, slot, sem, gather_sem, along_y):
        settle(incoming, sem)
        for s in range(16):
            for part in range(2):
                stage[2 * s:2 * s + 2, part * CHUNK:(part + 1) * CHUNK] = incoming[s, part].astype(F32)
        for side in range(2):
            own = slice(side * 128, side * 128 + 128), slice(CHUNK + side * 128, CHUNK + side * 128 + 128)
            gathered[side, slot] = jnp.concatenate([stage[:, own[0]], stage[:, own[1]]], axis=1).astype(BF)

        for side in range(2):
            for step in FAR:
                device = at(x, around(y, step), c, z) if along_y else at(x, y, c, around(z, step))
                push(gathered.at[side, slot], gathered.at[side, slot], send3, gather_sem.at[side], device)

    @pl.when(live_p)
    def _():
        collect(in_p, all_p, y, in_sem.at[0], p_sem, True)

    @pl.when(live_q)
    def _():
        collect(in_q, all_q, z, in_sem.at[1], q_sem, False)

    lane = iota((W, 128), 1)

    pltpu.make_async_copy(rvec_hbm, rvec, small_sem.at[0]).wait()
    pltpu.make_async_copy(degen_hbm, degen, small_sem.at[1]).wait()
    settle(k_p.at[pl.ds(0, 56)], k2_sem.at[0])
    settle(k_q.at[pl.ds(0, 56)], k2_sem.at[1])
    lattice_rows = iota((128, NR), 0)
    rv = rvec[...].astype(F32)
    lattice = jnp.where(
        lattice_rows < 8, rv[0:1],
        jnp.where(lattice_rows < 16, rv[1:2], jnp.where(lattice_rows < 24, rv[2:3], 0.0)),
    )
    weight = degen[...].astype(F32)

    @pl.when(live_p)
    def _():
        fold_table(k_p, lattice.astype(BF), 1.0 / weight, tab_p)

    @pl.when(live_q)
    def _():
        col = iota((NR, NR), 1)
        source = (
            lax.rem(lax.div(col, 2), 8) * 32 + lax.rem(lax.div(col, 16), 2) * 16
            + lax.div(col, 32) * 2 + lax.rem(col, 2)
        )
        swap = (iota((NR, NR), 0) == source).astype(F32).astype(BF)
        moved = dot(lattice.astype(BF), swap).astype(BF)
        weights = dot(jnp.broadcast_to(weight, (8, NR)).astype(BF), swap)[0:1]
        fold_table(k_q, moved, 1.0 / weights, tab_q)

    def deliver(chunk, out, along_z, side, half):
        dst = full.at[half, x, chunk, side]
        sem = full_sem.at[half]

        def one(step, some):
            ring = around(z if along_z else y, step)
            for px, pc, pxc in some:
                device = at(px, y, pc, ring) if along_z else at(px, ring, pc, z)
                push(out.at[half, side, pxc * 8 + ring], dst, send3, sem, device)

        for step in FAR:
            one(step, columns)
        one(0, columns[:-1])
        keep(out.at[half, side, xc * 8 + (z if along_z else y)], dst, sem)

    def serve_p(side, half):
        @pl.when(live_p)
        def _():
            if half == 0:
                settle(all_p.at[side, pl.ds(0, 7)], p_sem.at[side])
            transform(tab_p, all_p, out_p, side, half)
            deliver(chunk_p, out_p, True, side, half)

    def serve_q(side, half):
        @pl.when(live_q)
        def _():
            if half == 0:
                settle(all_q.at[side, pl.ds(0, 7)], q_sem.at[side])
            transform(tab_q, all_q, out_q, side, half)
            deliver(chunk_q, out_q, False, side, half)

    for side in range(2):
        for half in range(2):
            serve_p(side, half)
            serve_q(side, half)

    pltpu.make_async_copy(vectors, vec, vec_sem).wait()
    for part in range(2):
        def put(i, val, part=part):
            mats[part, i * KPT:(i + 1) * KPT, :] = val

        matrix_rows(lambda t, part=part: vec[:, part * HALF + t * 128: part * HALF + (t + 1) * 128].astype(F32), put)

    def eigen(k):
        vr = mats[0, pl.ds(k, W, stride=KPT), :]
        vi = mats[1, pl.ds(k, W, stride=KPT), :]
        gap = jnp.zeros((48, 256), BF)
        right[k, 0:W, :] = jnp.concatenate([vr, vi], axis=1).astype(BF)
        right[k, W:128, :] = gap
        right[k, 128:128 + W, :] = jnp.concatenate([-vi, vr], axis=1).astype(BF)
        right[k, 128 + W:, :] = gap
        fill = jnp.zeros((48, 128), F32)
        tr = jnp.transpose(jnp.concatenate([vr, fill], axis=0))[:W]
        ti = jnp.transpose(jnp.concatenate([vi, fill], axis=0))[:W]
        left[k] = paired(tr, ti).astype(BF)

    def paired(re, im):
        moved = pltpu.roll(im, W, 1)
        return jnp.concatenate([jnp.where(lane < W, re, moved), moved[:, :2 * W - 128]], axis=1)

    each(KPT, eigen)

    sub = iota((W, 128), 0)

    def rotate(half):
        settle(full.at[half], full_sem.at[half])

        def rebuild(o):
            def put(i, val):
                mats[o, i * KPT:(i + 1) * KPT, :] = val

            matrix_rows(lambda t: full[half, o, t // 2, t % 2].astype(F32), put)

        for o in range(4):
            rebuild(o)
        group = range(4)
        prods = []
        for k in group:
            ops = [
                jnp.concatenate(
                    [mats[o, pl.ds(k, W, stride=KPT), :], mats[o, pl.ds(4 + k, W, stride=KPT), :]], axis=1
                ).astype(BF)
                for o in range(4)
            ]
            prods.append(dot(jnp.concatenate(ops, axis=0), right[half * 4 + k]).astype(BF))
        rots = [[] for _ in group]
        for o in range(4):
            for k in group:
                re = prods[k][o * W:(o + 1) * W, :128]
                im = prods[k][o * W:(o + 1) * W, 128:]
                stacked = jnp.concatenate(
                    [jnp.concatenate([re, im], axis=1), jnp.concatenate([im, -re], axis=1)], axis=0
                )
                rots[k].append(dot(left[half * 4 + k], stacked).astype(BF))
        hams, weights = [], []
        for k in group:
            ham_re, ham_im = rots[k][0][:, :128].astype(F32), rots[k][0][:, 128:].astype(F32)
            diag = jnp.where(sub == lane, ham_re, 0.0)
            down = 1.0 / (1.0 + jnp.exp(jnp.sum(diag, axis=1, keepdims=True) * (1.0 / SMEARING)))
            along = 1.0 / (1.0 + jnp.exp(jnp.sum(diag, axis=0, keepdims=True) * (1.0 / SMEARING)))
            weights.append((1.0 - down) * along)
            hams.append(paired(ham_re, ham_im).astype(BF))
        products = [[] for _ in group]
        turned = [[] for _ in group]
        fill = jnp.zeros((48, 128), F32)
        for b in range(3):
            for k in group:
                re, im = rots[k][b + 1][:, :128], rots[k][b + 1][:, 128:]
                stacked = jnp.concatenate(
                    [jnp.concatenate([re, im], axis=1), jnp.concatenate([-im, re], axis=1)], axis=0
                )
                products[k].append(dot(hams[k], stacked))
                turned[k].append((
                    jnp.transpose(jnp.concatenate([re.astype(F32), fill], axis=0))[:W],
                    jnp.transpose(jnp.concatenate([im.astype(F32), fill], axis=0))[:W],
                ))
        spot8 = iota((KPT, 128), 0)
        for comp, (a, b) in enumerate(((1, 2), (2, 0), (0, 1))):
            found = jnp.zeros((KPT, 128), F32)
            for k in group:
                terms = (
                    turned[k][a][0] * products[k][b][:, 128:] + turned[k][a][1] * products[k][b][:, :128]
                    - turned[k][b][0] * products[k][a][:, 128:] - turned[k][b][1] * products[k][a][:, :128]
                ) * weights[k]
                found = jnp.where(spot8 == half * 4 + k, jnp.sum(terms, axis=0, keepdims=True) * (1.0 / W), found)
            stage[comp * KPT:(comp + 1) * KPT, 0:128] = stage[comp * KPT:(comp + 1) * KPT, 0:128] + found

    stage[...] = jnp.zeros_like(stage)
    each(2, rotate)
    spot = iota((1, 128), 1)
    part = jnp.zeros((1, 128), F32)
    for comp in range(3):
        sumk = jnp.sum(stage[comp * KPT:(comp + 1) * KPT, 0:128], axis=0, keepdims=True)
        part = part + jnp.where(spot == comp, jnp.sum(sumk, axis=1, keepdims=True), 0.0)

    sums[xc * 8 + z] = part

    def tell(step, some):
        ring = around(z, step)
        for px, pc, _ in some:
            push(sums.at[xc * 8 + z], sums.at[xc * 8 + z], sum_send, sum_sem.at[0], at(px, y, pc, ring))

    for step in FAR:
        tell(step, columns)
    tell(0, columns[:-1])
    eye = iota((KPT, 128), 0) == iota((KPT, 128), 1)
    for comp in range(3):
        column = jnp.sum(stage[comp * KPT:(comp + 1) * KPT, 0:128], axis=1, keepdims=True)
        result[comp:comp + 1] = jnp.sum(jnp.where(eye, column, 0.0), axis=0, keepdims=True)
    settle(sums.at[pl.ds(0, 63)], sum_sem.at[0])
    sums2[y] = jnp.sum(sums[:, 0, :], axis=0, keepdims=True)
    for step in FAR:
        push(sums2.at[y], sums2.at[y], sum_send, sum_sem.at[1], at(x, around(y, step), c, z))
    settle(sums2.at[pl.ds(0, 7)], sum_sem.at[1])
    part = jnp.sum(sums2[:, 0, :], axis=0, keepdims=True)
    result[3:4] = part * (1.0 / KPOINTS)

    settle(sums.at[pl.ds(0, 63)], sum_send)
    settle(sums2.at[pl.ds(0, 7)], sum_send)
    settle(k_p.at[pl.ds(0, 14)], send1)
    settle(k_p.at[pl.ds(0, 56)], send1)
    settle(k_p.at[pl.ds(0, 56)], send1)

    settle(in_p.at[pl.ds(0, 12)], send2)

    @pl.when(jnp.logical_not(live_p))
    def _():
        settle(in_p.at[pl.ds(0, 1)], send2)

    settle(in_q.at[pl.ds(0, 11)], send2)

    @pl.when(jnp.logical_not(live_q))
    def _():
        settle(in_q.at[pl.ds(0, 1)], send2)

    @pl.when(live_p)
    def _():
        for side in range(2):
            settle(all_p.at[side, pl.ds(0, 7)], send3)
        for half in range(2):
            for side in range(2):
                settle(out_p.at[half, side, pl.ds(0, 63)], send3)

    @pl.when(live_q)
    def _():
        for side in range(2):
            settle(all_q.at[side, pl.ds(0, 7)], send3)
        for half in range(2):
            for side in range(2):
                settle(out_q.at[half, side, pl.ds(0, 63)], send3)


def per_device(kgrid, rvec, degen, operators, vectors):
    vmem = pl.BlockSpec(memory_space=pltpu.VMEM)
    anywhere = pl.BlockSpec(memory_space=pl.ANY)
    dma = pltpu.SemaphoreType.DMA
    result = pl.pallas_call(
        body,
        out_shape=pltpu.VMEM((8, 128), F32),
        in_specs=[anywhere] * 5,
        out_specs=vmem,
        scratch_shapes=[
            pltpu.VMEM((3, KPT), jnp.int32),
            pltpu.VMEM((3, NR), jnp.int32),
            pltpu.VMEM((1, NR), jnp.int32),
            pltpu.VMEM((1, 2, 2 * HALF), BF),
            pltpu.VMEM((KPT, 2 * HALF), BF),
            pltpu.VMEM((1, 1, 128), F32),
            pltpu.VMEM((64, 1, 128), F32),
            pltpu.VMEM((64, 1, 128), F32),
            pltpu.VMEM((16, 2, 2, CHUNK), BF),
            pltpu.VMEM((16, 2, 2, CHUNK), BF),
            pltpu.VMEM((32, 2 * CHUNK), F32),
            pltpu.VMEM((2, RING, 32, CHUNK), BF),
            pltpu.VMEM((2, RING, 32, CHUNK), BF),
            pltpu.VMEM((1024, 2 * NR), BF),
            pltpu.VMEM((1024, 2 * NR), BF),
            pltpu.VMEM((2, 2, 64, KPT, 128), BF),
            pltpu.VMEM((2, 2, 64, KPT, 128), BF),
            pltpu.VMEM((2, 4, CHUNKS, 2, KPT, 128), BF),
            pltpu.VMEM((4, W * KPT, 128), F32),
            pltpu.VMEM((KPT, 256, 256), BF),
            pltpu.VMEM((KPT, W, 2 * W), BF),
            pltpu.VMEM((64, 1, 128), F32),
            pltpu.VMEM((8, 1, 128), F32),
            dma, dma, dma, dma((2,)), dma((2,)), dma((2,)), dma((2,)), dma((2,)), dma((2,)), dma, dma, dma((2,)), dma, dma((2,)), dma,
        ],
        compiler_params=pltpu.CompilerParams(
            collective_id=0, has_side_effects=True, vmem_limit_bytes=56 * 1024 * 1024
        ),
        name="orbital",
    )(kgrid, rvec, degen.reshape(1, NR), operators, vectors)
    return result[0:3, 0:KPT], result[3, 0:3]


def solution(mesh):
    return jax.shard_map(
        per_device,
        mesh=mesh,
        in_specs=(P(None, ("ka", "op", "row")), P(), P(), P("op", ("ka", "row"), None), P(("ka", "op", "row"), None)),
        out_specs=(P(None, ("ka", "op", "row")), P()),
        check_vma=False,
    )
```
